32 devices in a mesh: wave: 4 (over y, x), event: 8 (over z, core).
Axes of the slice: x: 2, y: 2, z: 4, core: 2. Of those that a mesh axis runs over, the one named last changes fastest.
Arguments:
- latent: bfloat16 [8, 512, 2048], P(None, 'wave', 'event'), may hold values from -6 to 6
- basis: bfloat16 [262144, 512], P('event', 'wave'), may hold values from -0.29882812 to 0.29882812
- event_bin: int32 [8, 32768], P('event'), may hold values from 0 to 255, never falling along the last dimension, each value on 1 to 512 neighbouring positions
- length: float32 [512, 2048], P('wave', 'event'), may hold values from 0.01 to 0.08
- amplitude_scale: float32 [512, 2048], P('wave', 'event'), may hold values from 0.3 to 1
- yield_norm: float32 [512, 2048], P('wave', 'event'), may hold values from 0.5 to 2
- bin_coords: float32 [2, 2048], replicated, may hold values from 0 to 1
Outputs:
- grad_latent: float32 [8, 512, 2048], P(None, 'wave', 'event')
The draws below stay inside these ranges and needn't reach their ends.
Inputs may be any that keep to these rules, and one draw needn't show every extreme that they name: `event_bin`: along each block's events, bin numbers never fall and every one of the block's bins holds at least one event.
All inputs are finite; a program needn't handle non-finite values.
Results may differ from the reference program's by a relative error of at most 0.0024.
Values may be sent and summed in bfloat16 or wider, within the bound.
A program may use at most 256 MiB of HBM per device.

```python
import math
import jax
import jax.numpy as jnp
import numpy as np
from jax import lax

B = 2048
W = 512
S = 8
EV_DEV = 32768
NBLOCKS = 8
EVENTS = 262144
N_EVENT = 8


def block_scale(own_key, shape, split, least, largest):
    def one(position, blocks):
        steps = jax.random.uniform(jax.random.fold_in(jax.random.fold_in(own_key, 6), position), (blocks,), jnp.float32, least / len(split), largest / len(split))
        return jnp.repeat(jnp.exp(steps), shape[position] // blocks).reshape((-1,) + (1,) * (len(shape) - position - 1))

    gain = one(*split[0])
    for cut in split[1:]:
        gain = gain * one(*cut)
    return gain


def length_profile(amount, total, most, lean):
    portions = [(1 << 20) // math.isqrt(grade ** lean) + 1 for grade in range(2, amount + 1)]
    spare, counts = total - most - (amount - 1), [1] * (amount - 1)
    while spare > 0:
        candidates = [i for i in range(amount - 1) if counts[i] < most]
        pool, budget = sum([portions[i] for i in candidates]), spare
        for i in candidates:
            addition = min(most - counts[i], max(1, budget * portions[i] // pool), spare)
            counts[i] = counts[i] + addition
            spare = spare - addition
    return np.array([most] + counts)


def uneven(stream_key, amount, total, bound, skew):
    if amount == 2:
        one = jax.random.randint(stream_key, (), max(1, total - bound), min(bound, total - 1) + 1)
        return jnp.stack([one, total - one])
    tallies = jnp.asarray(length_profile(amount, total, bound, skew), jnp.int32)
    couples = (amount - 1) // 2
    source_of, receiver = tallies[1:1 + 2 * couples:2], tallies[2:2 + 2 * couples:2]
    slack = jnp.minimum(source_of - 1, bound - receiver)
    passed = jax.random.randint(jax.random.fold_in(stream_key, 1), (couples,), 0, 1 << 20) % (slack + 1)
    tallies = tallies.at[1:1 + 2 * couples:2].set(source_of - passed).at[2:2 + 2 * couples:2].set(receiver + passed)
    return tallies[jax.random.permutation(jax.random.fold_in(stream_key, 2), amount)]


def gaussian(rng, dims, width, reach, cuts=(), held_as=jnp.bfloat16):
    factor_of = block_scale(rng, dims, cuts, -0.22, 0.18) if cuts else 1.0
    drawn = jax.random.normal(rng, dims, jnp.float32) * width * factor_of
    return jnp.minimum(jnp.maximum(drawn, -reach), reach).astype(held_as)


def setup_inputs(seed: int = 0) -> dict:
    key_of = jax.random.split(jax.random.key(seed), 8)
    return {
        "latent": gaussian(key_of[0], (S, W, B), 1.0, 6.0, ((1, 4), (2, 8))),
        "basis": gaussian(key_of[1], (EVENTS, W), 0.05, 0.29882812, ((0, 8), (1, 4))),
        "event_bin": jax.vmap(lambda own: jnp.searchsorted(jnp.cumsum(uneven(own, B // N_EVENT, EV_DEV, min(4 * EV_DEV // (B // N_EVENT), EV_DEV - B // N_EVENT + 1), 2)), jnp.arange(EV_DEV), side="right"))(jax.random.split(key_of[2], NBLOCKS)).reshape((NBLOCKS, EV_DEV)).astype(jnp.int32),
        "length": jnp.clip(jnp.exp(math.log(0.08) - 2.0794415 * jax.random.uniform(key_of[3], (W, B), jnp.float32) ** block_scale(key_of[3], (W, B), ((0, 4), (1, 8)), -0.2, 0.2)), 0.01, 0.08),
        "amplitude_scale": jnp.clip(jnp.exp(math.log(1.0) - 1.2039728 * jax.random.uniform(key_of[4], (W, B), jnp.float32) ** block_scale(key_of[4], (W, B), ((0, 4), (1, 8)), -0.2, 0.2)), 0.3, 1.0),
        "yield_norm": jnp.clip(jnp.exp(math.log(2.0) - 1.3862944 * jax.random.uniform(key_of[5], (W, B), jnp.float32) ** block_scale(key_of[5], (W, B), ((0, 4), (1, 8)), -0.2, 0.2)), 0.5, 2.0),
        "bin_coords": jnp.clip(jax.random.uniform(key_of[6], (2, B), jnp.float32, 0.0, 1.0), 0.0, 1.0),
    }


def gibbs(rows_xy, cols_xy, len_rows, amp_rows, len_cols, amp_cols):
    diff_x = rows_xy[0][:, None] - cols_xy[0][None, :]
    diff_y = rows_xy[1][:, None] - cols_xy[1][None, :]
    dist = diff_x * diff_x + diff_y * diff_y
    left = len_rows[:, :, None]
    right = len_cols[:, None, :]
    spread = left * left + right * right
    return amp_rows[:, :, None] * amp_cols[:, None, :] * jnp.sqrt(2.0 * (left * right) / spread) * jnp.exp(-dist / spread)

def reference(latent, basis, event_bin, length, amplitude_scale, yield_norm, bin_coords):
    rows = B // N_EVENT

    def wave_kernel(w_index):
        len_wave = length[w_index][None]
        amp_wave = amplitude_scale[w_index][None]
        return gibbs(bin_coords, bin_coords, len_wave, amp_wave, len_wave, amp_wave)[0].astype(jnp.bfloat16)

    def forward_wave(w_index):
        kern = wave_kernel(w_index)
        return jnp.dot(kern, latent[:, w_index, :].T, preferred_element_type=jnp.float32)
    amps = lax.map(forward_wave, jnp.arange(W, dtype=jnp.int32))
    amplitude = jnp.transpose(amps, (2, 0, 1)).astype(jnp.bfloat16)
    basis_blocks = basis.reshape(NBLOCKS, EV_DEV, W)

    def block_sums(pieces):
        blk, psi, seg = pieces
        local = lax.dynamic_slice_in_dim(amplitude, (blk * rows).astype(jnp.int32), rows, 2).astype(jnp.float32)
        picked = jnp.transpose(local, (2, 0, 1))[seg]
        psi_wide = psi.astype(jnp.float32)
        field = lax.optimization_barrier(jnp.sum(picked * psi_wide[:, None, :], axis=2))
        weight = -2.0 * field / (1.0 + field * field) / S
        terms = (weight[:, :, None] * psi_wide[:, None, :]).astype(jnp.bfloat16)
        terms = lax.optimization_barrier(terms).astype(jnp.float32)
        return jax.ops.segment_sum(terms, seg, num_segments=rows)
    sums = lax.map(block_sums, (jnp.arange(NBLOCKS, dtype=jnp.int32), basis_blocks, event_bin))
    sums = sums.reshape(B, S, W)
    yield_term = 2.0 / S * amplitude.astype(jnp.float32) * yield_norm[None]
    bin_grad = (sums + jnp.transpose(yield_term, (2, 0, 1))).astype(jnp.bfloat16)

    def backward_wave(w_index):
        kern = wave_kernel(w_index)
        return jnp.dot(kern, bin_grad[:, :, w_index], preferred_element_type=jnp.float32)
    grads = lax.map(backward_wave, jnp.arange(W, dtype=jnp.int32))
    return jnp.transpose(grads, (2, 0, 1)) + latent.astype(jnp.float32)
```

```python
import functools
import math

import jax
import jax.numpy as jnp
from jax import lax
from jax.experimental import pallas as pl
from jax.experimental.pallas import tpu as pltpu
from jax.sharding import PartitionSpec as P

TILE = 256
LANES = 128
CHUNK = 1024
GROUP = 16
BATCHES = 8
MESH = pl.DeviceIdType.MESH
NN = (((1,), (0,)), ((), ()))
NT = (((1,), (1,)), ((), ()))


def dot(a, b, dims):
    return lax.dot_general(a, b, dims, preferred_element_type=jnp.float32)


def spread_rows(dst, read, total):
    for k in range(total // LANES):
        row = read(k * LANES)
        dst[pl.ds(k * LANES, LANES), :] = jnp.broadcast_to(row, (LANES, LANES)).T


def gather_pieces(dst, src, pieces, width):
    for k in range(pieces):
        block, lane = (k * width) // TILE, (k * width) % TILE
        dst[block, :, lane : lane + width] = src(k)


def wide(column):
    return jnp.concatenate([column] * (TILE // LANES), axis=1)


def tile_pairs(blocks):
    return [(i, j) for i in range(blocks) for j in range(i, blocks)]


def add(held, term):
    return term if held is None else held + term


def multiply(sums, vec, tile, i, j):
    sums[j] = add(sums[j], dot(vec[i], tile, NN))
    if j > i:
        sums[i] = add(sums[i], dot(vec[j], tile, NT))


def keep_pieces(dst, slot, sums, pieces, width):
    for k in range(pieces):
        block, lane = (k * width) // TILE, (k * width) % TILE
        dst[slot, k] = sums[block][:, lane : lane + width].astype(dst.dtype)


def around(axis, count):
    me = lax.axis_index(axis)
    return me, [lax.rem(me + d, count) for d in range(1, count)]


def remote(axis, peer, src, dst, send, recv):
    return pltpu.make_async_remote_copy(
        src_ref=src,
        dst_ref=dst,
        send_sem=send,
        recv_sem=recv,
        device_id={axis: peer},
        device_id_type=MESH,
    )


def inward(axis, count, batch, sources, targets, send, recv):
    me, peers = around(axis, count)

    def copies(q):
        size = sources[0].shape[1] // batch
        at = pl.ds(q * size, size)
        return [
            remote(axis, peer, src.at[peer, at], dst.at[me, at], send.at[a, q, d], recv.at[a, q, d])
            for a, (src, dst) in enumerate(zip(sources, targets))
            for d, peer in enumerate(peers)
        ]

    return copies


def outward(axis, count, stage, landed, send, recv):
    me, peers = around(axis, count)

    def copies(w):
        return [
            remote(axis, peer, stage.at[w, peer], landed.at[me, w], send.at[w, d], recv.at[w, d])
            for d, peer in enumerate(peers)
        ]

    return copies


def open_batches(axis, count, batch, sources, targets, copies):
    me, _ = greet(axis, count)
    for q in range(batch):
        for copy in copies(q):
            copy.start()
    for src, dst in zip(sources, targets):
        dst[me] = src[me]


def close_all(own, batch, copies_in, copies_out):
    def sent(q, _):
        for copy in copies_in(q):
            copy.wait_send()
        return 0

    def done(w, _):
        for copy in copies_out(w):
            copy.wait()
        return 0

    lax.fori_loop(0, batch, sent, 0)
    lax.fori_loop(0, own, done, 0)


def split_scaled(vec, value, scale, at):
    whole = value.astype(jnp.float32) * scale
    high = whole.astype(vec.dtype)
    low = (whole - high.astype(jnp.float32)).astype(vec.dtype)
    vec[at] = jnp.concatenate([high, low], axis=0)


def joined(sums, scale, samples):
    return [
        (part[:samples] + part[samples:]) * scale(block) for block, part in enumerate(sums)
    ]


def forward_kernel(
    axis, pieces, width, own, batch,
    coords, profile, latent, kern, amp, kept,
    dist, col_x, col_y, prof, later, draw, vec, prof_all, draws_all, stage, landed,
    in_send, in_recv, out_send, out_recv,
):
    total = pieces * width
    blocks = total // TILE
    samples = latent.shape[2]
    step = 64
    per = own // batch
    w = pl.program_id(0)
    sources, targets = (profile, latent), (prof_all, draws_all)
    copies_in = inward(axis, pieces, batch, sources, targets, in_send, in_recv)
    copies_out = outward(axis, pieces, stage, landed, out_send, out_recv)
    me = lax.axis_index(axis)

    @pl.when(w == 0)
    def _():
        open_batches(axis, pieces, batch, sources, targets, copies_in)
        spread_rows(col_x, lambda k: coords[0:1, k : k + LANES], total)
        spread_rows(col_y, lambda k: coords[1:2, k : k + LANES], total)

        def over_i(i, t0):
            def over_j(j, t):
                col = pl.ds(pl.multiple_of(j * TILE, TILE), TILE)
                x_c, y_c = coords[0:1, col], coords[1:2, col]
                for r in range(0, TILE, step):
                    row = pl.ds(pl.multiple_of(i * TILE + r, step), step)
                    dx = wide(col_x[row, :]) - x_c
                    dy = wide(col_y[row, :]) - y_c
                    dist[t, r : r + step, :] = (dx * dx + dy * dy) * (-math.log2(math.e))
                return t + 1

            return lax.fori_loop(i, blocks, over_j, t0)

        lax.fori_loop(0, blocks, over_i, 0)
        for copy in copies_in(0):
            copy.wait_recv()
        gather_pieces(later, lambda k: prof_all[k, 0], pieces, width)
        spread_rows(col_x, lambda k: later[k // TILE, 0:1, k % TILE : k % TILE + LANES], total)

    @pl.when(w > 0)
    def _():
        for copy in copies_out(w - 1):
            copy.start()
        landed[me, w - 1] = stage[w - 1, me]

    @pl.when(jnp.logical_and(w + 1 < own, lax.rem(w + 1, per) == 0))
    def _():
        for copy in copies_in((w + 1) // per):
            copy.wait_recv()

    @pl.when(w < own)
    def _():
        after = jnp.minimum(w + 1, own - 1)
        gather_pieces(prof, lambda k: prof_all[k, w], pieces, width)
        gather_pieces(later, lambda k: prof_all[k, after], pieces, width)
        gather_pieces(draw, lambda k: draws_all[k, w], pieces, width)
        kept[w] = prof[...]
        for j in range(blocks):
            split_scaled(vec, draw[j], prof[j, 1:2, :], j)
        sums = [None] * blocks
        for t, (i, j) in enumerate(tile_pairs(blocks)):
            l_c = prof[j, 0:1, :]
            strips = []
            for r in range(0, TILE, step):
                row = pl.ds(i * TILE + r, step)
                root = lax.rsqrt(wide(col_x[row, :]) + l_c)
                power = jnp.exp2(dist[t, r : r + step, :] * (root * root))
                strip = (root * power).astype(jnp.bfloat16)
                kern[0, t, r : r + step, :] = strip
                strips.append(strip)
            multiply(sums, vec, jnp.concatenate(strips, axis=0), i, j)
            if j == blocks - 1:
                for k in range(0, TILE, LANES):
                    row = later[i, 0:1, k : k + LANES]
                    at = pl.ds(i * TILE + k, LANES)
                    col_x[at, :] = jnp.broadcast_to(row, (LANES, LANES)).T
        sums = joined(sums, lambda j: prof[j, 1:2, :], samples)
        keep_pieces(stage, w, sums, pieces, width)

    @pl.when(w == own)
    def _():
        close_all(own, batch, copies_in, copies_out)
        amp[...] = landed[...]


def backward_kernel(
    axis, pieces, width, own, batch,
    kern, grad, prof, out,
    draw, vec, grad_all, stage, landed, in_send, in_recv, out_send, out_recv,
):
    total = pieces * width
    blocks = total // TILE
    samples = grad.shape[2]
    w = pl.program_id(0)
    copies_in = inward(axis, pieces, batch, (grad,), (grad_all,), in_send, in_recv)
    copies_out = outward(axis, pieces, stage, landed, out_send, out_recv)
    me = lax.axis_index(axis)

    @pl.when(w == 0)
    def _():
        open_batches(axis, pieces, batch, (grad,), (grad_all,), copies_in)

    @pl.when(w > 0)
    def _():
        for copy in copies_out(w - 1):
            copy.start()
        landed[me, w - 1] = stage[w - 1, me]

    @pl.when(jnp.logical_and(w < own, lax.rem(w, own // batch) == 0))
    def _():
        for copy in copies_in(w // (own // batch)):
            copy.wait_recv()

    @pl.when(w < own)
    def _():
        gather_pieces(draw, lambda k: grad_all[k, w], pieces, width)
        for j in range(blocks):
            split_scaled(vec, draw[j], prof[w, j, 1:2, :], j)
        sums = [None] * blocks
        for t, (i, j) in enumerate(tile_pairs(blocks)):
            multiply(sums, vec, kern[0, t], i, j)
        sums = joined(sums, lambda j: prof[w, j, 1:2, :], samples)
        keep_pieces(stage, w, sums, pieces, width)

    @pl.when(w == own)
    def _():
        close_all(own, batch, copies_in, copies_out)
        out[...] = landed[...]


def field_kernel(samples, inner, first, last, rows, basis, label, field):
    base = pl.program_id(0) * inner

    def group(c, start):
        at = pl.ds(c * CHUNK, CHUNK)
        part = rows[pl.ds(pl.multiple_of(start * samples, 2 * samples), GROUP * samples), :]
        full = dot(part, basis[at, :], NT)
        own = jnp.broadcast_to(label[:, at], (samples, CHUNK)) - start
        total = jnp.zeros((samples, CHUNK), jnp.float32)
        for b in range(GROUP):
            total = total + jnp.where(own == b, full[b * samples : (b + 1) * samples, :], 0.0)
        return total

    starts = [first[base + c] // 2 * 2 for c in range(inner)]
    totals = [group(c, starts[c]) for c in range(inner)]
    for c in range(inner):
        trips = (last[base + c] - starts[c]) // GROUP + 1

        def over(k, total, c=c):
            return total + group(c, starts[c] + k * GROUP)

        total = lax.fori_loop(1, trips, over, totals[c])
        field[0, :, c * CHUNK : (c + 1) * CHUNK] = total.astype(field.dtype)


def sums_kernel(samples, inner, first, last, weight, basis, label, sums):
    base = pl.program_id(0) * inner

    @pl.when(pl.program_id(0) == 0)
    def _():
        sums[...] = jnp.zeros_like(sums)

    def group(c, start):
        at = pl.ds(c * CHUNK, CHUNK)
        own = jnp.broadcast_to(label[:, at], (samples, CHUNK)) - start
        value = weight[0, :, at].astype(jnp.float32)
        full = jnp.concatenate([jnp.where(own == b, value, 0.0) for b in range(GROUP)], axis=0)
        return dot(full.astype(jnp.bfloat16), basis[at, :], NN)

    def put(start, term):
        sums[pl.ds(pl.multiple_of(start * samples, 2 * samples), GROUP * samples), :] += term

    starts = [first[base + c] // 2 * 2 for c in range(inner)]
    terms = [group(c, starts[c]) for c in range(inner)]
    for c in range(inner):
        put(starts[c], terms[c])
    for c in range(inner):
        trips = (last[base + c] - starts[c]) // GROUP + 1

        def over(k, _, c=c):
            put(starts[c] + k * GROUP, group(c, starts[c] + k * GROUP))
            return 0

        lax.fori_loop(1, trips, over, 0)


def greet(axis, count):
    me = lax.axis_index(axis)
    peers = [lax.rem(me + d, count) for d in range(1, count)]
    barrier = pltpu.get_barrier_semaphore()
    for peer in peers:
        pl.semaphore_signal(barrier, inc=1, device_id={axis: peer}, device_id_type=MESH)
    pl.semaphore_wait(barrier, count - 1)
    return me, peers


def weight_kernel(axis, count, samples, partial, weight, landed, made, send, recv, local):
    me, peers = greet(axis, count)
    copies = []
    for d, peer in enumerate(peers):
        copy = pltpu.make_async_remote_copy(
            src_ref=partial.at[peer],
            dst_ref=landed.at[d],
            send_sem=send.at[0, d],
            recv_sem=recv.at[0, d],
            device_id={axis: peer},
            device_id_type=MESH,
        )
        copy.start()
        copies.append(copy)
    for copy in copies:
        copy.wait()
    total = partial[me].astype(jnp.float32)
    for d in range(count - 1):
        total = total + landed[d].astype(jnp.float32)
    made[...] = (-2.0 * total / (1.0 + total * total) / samples).astype(made.dtype)
    keep = pltpu.make_async_copy(made, weight.at[me], local)
    keep.start()
    keep.wait()
    copies = []
    for d, peer in enumerate(peers):
        copy = pltpu.make_async_remote_copy(
            src_ref=weight.at[me],
            dst_ref=weight.at[me],
            send_sem=send.at[1, d],
            recv_sem=recv.at[1, d],
            device_id={axis: peer},
            device_id_type=MESH,
        )
        copy.start()
        copies.append(copy)
    for copy in copies:
        copy.wait()


def share_weight(axis, count, ident, samples, partial):
    vmem = pl.BlockSpec(memory_space=pltpu.VMEM)
    shape, dtype = partial.shape, partial.dtype
    return pl.pallas_call(
        functools.partial(weight_kernel, axis, count, samples),
        out_shape=jax.ShapeDtypeStruct(shape, dtype),
        in_specs=[vmem],
        out_specs=vmem,
        scratch_shapes=[
            pltpu.VMEM((count - 1,) + shape[1:], dtype),
            pltpu.VMEM(shape[1:], dtype),
            pltpu.SemaphoreType.DMA((2, count - 1)),
            pltpu.SemaphoreType.DMA((2, count - 1)),
            pltpu.SemaphoreType.DMA,
        ],
        compiler_params=pltpu.CompilerParams(
            collective_id=ident, has_side_effects=True, vmem_limit_bytes=12 << 20
        ),
        name="share_weight",
    )(partial)


def params(**more):
    return pltpu.CompilerParams(
        dimension_semantics=("arbitrary",), vmem_limit_bytes=60 << 20, **more
    )


def shards(count, splits, latent, basis, event_bin, length, amplitude_scale, yield_norm, bin_coords):
    samples, waves, width = latent.shape
    total = bin_coords.shape[1]
    own = waves // count
    blocks = total // TILE
    tiles = blocks * (blocks + 1) // 2
    f32, bf16 = jnp.float32, jnp.bfloat16

    profile = jnp.stack(
        [length * length, amplitude_scale * jnp.sqrt(math.sqrt(2.0) * length)], axis=1
    ).reshape(count, own, 2, width)
    draws = jnp.transpose(latent, (1, 0, 2)).reshape(count, own, samples, width)

    batch = math.gcd(own, BATCHES)
    vmem = pl.BlockSpec(memory_space=pltpu.VMEM)
    piece = jax.ShapeDtypeStruct((count, own, samples, width), bf16)
    kern_spec = pl.BlockSpec((1, tiles, TILE, TILE), lambda w: (jnp.minimum(w, own - 1), 0, 0, 0))
    stages = [
        pltpu.VMEM((own, count, samples, width), bf16),
        pltpu.VMEM((count, own, samples, width), bf16),
    ]

    def semaphores(arrays):
        return [pltpu.SemaphoreType.DMA((arrays, batch, count - 1))] * 2 + [
            pltpu.SemaphoreType.DMA((own, count - 1))
        ] * 2

    kern, amp, kept = pl.pallas_call(
        functools.partial(forward_kernel, "event", count, width, own, batch),
        out_shape=(
            jax.ShapeDtypeStruct((own, tiles, TILE, TILE), bf16),
            piece,
            jax.ShapeDtypeStruct((own, blocks, 2, TILE), f32),
        ),
        grid=(own + 1,),
        in_specs=[vmem, vmem, vmem],
        out_specs=(kern_spec, vmem, vmem),
        scratch_shapes=[
            pltpu.VMEM((tiles, TILE, TILE), f32),
            pltpu.VMEM((total, LANES), f32),
            pltpu.VMEM((total, LANES), f32),
            pltpu.VMEM((blocks, 2, TILE), f32),
            pltpu.VMEM((blocks, 2, TILE), f32),
            pltpu.VMEM((blocks, samples, TILE), bf16),
            pltpu.VMEM((blocks, 2 * samples, TILE), bf16),
            pltpu.VMEM((count, own, 2, width), f32),
            pltpu.VMEM((count, own, samples, width), bf16),
        ]
        + stages
        + semaphores(2),
        compiler_params=params(collective_id=0, has_side_effects=True),
        name="kern_forward",
    )(bin_coords, profile, draws)

    amp = amp.reshape(waves, samples, width)
    amp_rows = jnp.transpose(amp, (2, 1, 0)).reshape(width * samples, waves)
    amp_rows = jnp.pad(amp_rows, ((0, GROUP * samples), (0, 0)))

    events = basis.shape[0]
    block = min(events // splits, 4096)
    per = events // splits // block
    inner = block // CHUNK
    grouped = event_bin.reshape(events // CHUNK, CHUNK)
    first, last = grouped[:, 0], grouped[:, -1]
    basis_spec = pl.BlockSpec((block, waves), lambda e, *_: (e, 0))
    label_spec = pl.BlockSpec((1, block), lambda e, *_: (0, e))
    field_spec = pl.BlockSpec((1, samples, block), lambda e, *_: (e // per, 0, e % per))
    rows_spec = pl.BlockSpec(((width + GROUP) * samples, waves), lambda e, *_: (0, 0))
    field = pl.pallas_call(
        functools.partial(field_kernel, samples, inner),
        out_shape=jax.ShapeDtypeStruct((splits, samples, events // splits), bf16),
        grid_spec=pltpu.PrefetchScalarGridSpec(
            num_scalar_prefetch=2,
            grid=(events // block,),
            in_specs=[rows_spec, basis_spec, label_spec],
            out_specs=field_spec,
        ),
        compiler_params=params(),
        name="event_field",
    )(first, last, amp_rows, basis, event_bin)
    weight = share_weight("wave", splits, 2, samples, field)
    sums = pl.pallas_call(
        functools.partial(sums_kernel, samples, inner),
        out_shape=jax.ShapeDtypeStruct(((width + GROUP) * samples, waves), f32),
        grid_spec=pltpu.PrefetchScalarGridSpec(
            num_scalar_prefetch=2,
            grid=(events // block,),
            in_specs=[field_spec, basis_spec, label_spec],
            out_specs=rows_spec,
        ),
        compiler_params=params(),
        name="event_sums",
    )(first, last, weight, basis, event_bin)

    sums = jnp.transpose(sums[: width * samples].reshape(width, samples, waves), (2, 1, 0))
    grad = (sums + 2.0 / samples * amp.astype(f32) * yield_norm[:, None, :]).astype(bf16)
    pulled = pl.pallas_call(
        functools.partial(backward_kernel, "event", count, width, own, batch),
        out_shape=piece,
        grid=(own + 1,),
        in_specs=[kern_spec, vmem, vmem],
        out_specs=vmem,
        scratch_shapes=[
            pltpu.VMEM((blocks, samples, TILE), bf16),
            pltpu.VMEM((blocks, 2 * samples, TILE), bf16),
            pltpu.VMEM((count, own, samples, width), bf16),
        ]
        + stages
        + semaphores(1),
        compiler_params=params(collective_id=1, has_side_effects=True),
        name="kern_backward",
    )(kern, grad.reshape(count, own, samples, width), kept)
    pulled = pulled.reshape(waves, samples, width).astype(f32)
    return jnp.transpose(pulled, (1, 0, 2)) + latent.astype(f32)


def solution(mesh):
    placed = (
        P(None, "wave", "event"),
        P("event", "wave"),
        P("event", None),
        P("wave", "event"),
        P("wave", "event"),
        P("wave", "event"),
        P(),
    )
    return jax.shard_map(
        functools.partial(shards, mesh.shape["event"], mesh.shape["wave"]),
        mesh=mesh,
        in_specs=placed,
        out_specs=P(None, "wave", "event"),
        check_vma=False,
    )
```

```python
import functools
import math

import jax
import jax.numpy as jnp
from jax import lax
from jax.experimental import pallas as pl
from jax.experimental.pallas import tpu as pltpu
from jax.sharding import PartitionSpec as P

TILE = 256
LANES = 128
CHUNK = 1024
GROUP = 16
BATCHES = 8
HALVES = 2
MESH = pl.DeviceIdType.MESH
NN = (((1,), (0,)), ((), ()))
NT = (((1,), (1,)), ((), ()))


def dot(a, b, dims):
    return lax.dot_general(a, b, dims, preferred_element_type=jnp.float32)


def spread_rows(dst, read, total):
    for k in range(total // LANES):
        row = read(k * LANES)
        dst[pl.ds(k * LANES, LANES), :] = jnp.broadcast_to(row, (LANES, LANES)).T


def gather_pieces(dst, src, pieces, width):
    for k in range(pieces):
        block, lane = (k * width) // TILE, (k * width) % TILE
        dst[block, :, lane : lane + width] = src(k)


def wide(column):
    return jnp.concatenate([column] * (TILE // LANES), axis=1)


def tile_pairs(blocks):
    return [(i, j) for i in range(blocks) for j in range(i, blocks)]


def add(held, term):
    return term if held is None else held + term


def multiply(sums, vec, tile, i, j):
    sums[j] = add(sums[j], dot(vec[i], tile, NN))
    if j > i:
        sums[i] = add(sums[i], dot(vec[j], tile, NT))


def keep_pieces(dst, slot, sums, pieces, width):
    for k in range(pieces):
        block, lane = (k * width) // TILE, (k * width) % TILE
        dst[slot, k] = sums[block][:, lane : lane + width].astype(dst.dtype)


def around(axis, count):
    me = lax.axis_index(axis)
    return me, [lax.rem(me + d, count) for d in range(1, count)]


def remote(axis, peer, src, dst, send, recv):
    return pltpu.make_async_remote_copy(
        src_ref=src,
        dst_ref=dst,
        send_sem=send,
        recv_sem=recv,
        device_id={axis: peer},
        device_id_type=MESH,
    )


def inward(axis, count, batch, sources, targets, send, recv):
    me, peers = around(axis, count)

    def copies(q):
        size = sources[0].shape[1] // batch
        at = pl.ds(q * size, size)
        return [
            remote(axis, peer, src.at[peer, at], dst.at[me, at], send.at[a, q, d], recv.at[a, q, d])
            for a, (src, dst) in enumerate(zip(sources, targets))
            for d, peer in enumerate(peers)
        ]

    return copies


def outward(axis, count, stage, landed, send, recv):
    me, peers = around(axis, count)

    def copies(w):
        return [
            remote(axis, peer, stage.at[w, peer], landed.at[me, w], send.at[w, d], recv.at[w, d])
            for d, peer in enumerate(peers)
        ]

    return copies


def open_batches(axis, count, batch, sources, targets, copies):
    me, _ = greet(axis, count)
    for q in range(batch):
        for copy in copies(q):
            copy.start()
    for src, dst in zip(sources, targets):
        dst[me] = src[me]


def close_all(own, batch, copies_in, copies_out):
    def sent(q, _):
        for copy in copies_in(q):
            copy.wait_send()
        return 0

    def done(w, _):
        for copy in copies_out(w):
            copy.wait()
        return 0

    lax.fori_loop(0, batch, sent, 0)
    lax.fori_loop(0, own, done, 0)


def split_scaled(vec, value, scale, at):
    whole = value.astype(jnp.float32) * scale
    high = whole.astype(vec.dtype)
    low = (whole - high.astype(jnp.float32)).astype(vec.dtype)
    vec[at] = jnp.concatenate([high, low], axis=0)


def joined(sums, scale, samples):
    return [
        (part[:samples] + part[samples:]) * scale(block) for block, part in enumerate(sums)
    ]


def forward_kernel(
    axis, pieces, width, own, batch,
    coords, profile, latent, kern, amp, kept,
    dist, col_x, col_y, prof, later, draw, vec, prof_all, draws_all, stage, landed,
    in_send, in_recv, out_send, out_recv,
):
    total = pieces * width
    blocks = total // TILE
    samples = latent.shape[2]
    step = 64
    per = own // batch
    w = pl.program_id(0)
    sources, targets = (profile, latent), (prof_all, draws_all)
    copies_in = inward(axis, pieces, batch, sources, targets, in_send, in_recv)
    copies_out = outward(axis, pieces, stage, landed, out_send, out_recv)
    me = lax.axis_index(axis)

    @pl.when(w == 0)
    def _():
        open_batches(axis, pieces, batch, sources, targets, copies_in)
        spread_rows(col_x, lambda k: coords[0:1, k : k + LANES], total)
        spread_rows(col_y, lambda k: coords[1:2, k : k + LANES], total)

        def over_i(i, t0):
            def over_j(j, t):
                col = pl.ds(pl.multiple_of(j * TILE, TILE), TILE)
                x_c, y_c = coords[0:1, col], coords[1:2, col]
                for r in range(0, TILE, step):
                    row = pl.ds(pl.multiple_of(i * TILE + r, step), step)
                    dx = wide(col_x[row, :]) - x_c
                    dy = wide(col_y[row, :]) - y_c
                    dist[t, r : r + step, :] = (dx * dx + dy * dy) * (-math.log2(math.e))
                return t + 1

            return lax.fori_loop(i, blocks, over_j, t0)

        lax.fori_loop(0, blocks, over_i, 0)
        for copy in copies_in(0):
            copy.wait_recv()
        gather_pieces(later, lambda k: prof_all[k, 0], pieces, width)
        spread_rows(col_x, lambda k: later[k // TILE, 0:1, k % TILE : k % TILE + LANES], total)

    @pl.when(w > 0)
    def _():
        for copy in copies_out(w - 1):
            copy.start()
        landed[me, w - 1] = stage[w - 1, me]

    @pl.when(jnp.logical_and(w + 1 < own, lax.rem(w + 1, per) == 0))
    def _():
        for copy in copies_in((w + 1) // per):
            copy.wait_recv()

    @pl.when(w < own)
    def _():
        after = jnp.minimum(w + 1, own - 1)
        gather_pieces(prof, lambda k: prof_all[k, w], pieces, width)
        gather_pieces(later, lambda k: prof_all[k, after], pieces, width)
        gather_pieces(draw, lambda k: draws_all[k, w], pieces, width)
        kept[w] = prof[...]
        for j in range(blocks):
            split_scaled(vec, draw[j], prof[j, 1:2, :], j)
        sums = [None] * blocks
        for t, (i, j) in enumerate(tile_pairs(blocks)):
            l_c = prof[j, 0:1, :]
            strips = []
            for r in range(0, TILE, step):
                row = pl.ds(i * TILE + r, step)
                root = lax.rsqrt(wide(col_x[row, :]) + l_c)
                power = jnp.exp2(dist[t, r : r + step, :] * (root * root))
                strip = (root * power).astype(jnp.bfloat16)
                kern[0, t, r : r + step, :] = strip
                strips.append(strip)
            multiply(sums, vec, jnp.concatenate(strips, axis=0), i, j)
            if j == blocks - 1:
                for k in range(0, TILE, LANES):
                    row = later[i, 0:1, k : k + LANES]
                    at = pl.ds(i * TILE + k, LANES)
                    col_x[at, :] = jnp.broadcast_to(row, (LANES, LANES)).T
        sums = joined(sums, lambda j: prof[j, 1:2, :], samples)
        keep_pieces(stage, w, sums, pieces, width)

    @pl.when(w == own)
    def _():
        close_all(own, batch, copies_in, copies_out)
        amp[...] = landed[...]


def backward_kernel(
    axis, pieces, width, own, batch,
    kern, grad, prof, out,
    draw, vec, grad_all, stage, landed, in_send, in_recv, out_send, out_recv,
):
    total = pieces * width
    blocks = total // TILE
    samples = grad.shape[2]
    w = pl.program_id(0)
    copies_in = inward(axis, pieces, batch, (grad,), (grad_all,), in_send, in_recv)
    copies_out = outward(axis, pieces, stage, landed, out_send, out_recv)
    me = lax.axis_index(axis)

    @pl.when(w == 0)
    def _():
        open_batches(axis, pieces, batch, (grad,), (grad_all,), copies_in)

    @pl.when(w > 0)
    def _():
        for copy in copies_out(w - 1):
            copy.start()
        landed[me, w - 1] = stage[w - 1, me]

    @pl.when(jnp.logical_and(w < own, lax.rem(w, own // batch) == 0))
    def _():
        for copy in copies_in(w // (own // batch)):
            copy.wait_recv()

    @pl.when(w < own)
    def _():
        gather_pieces(draw, lambda k: grad_all[k, w], pieces, width)
        for j in range(blocks):
            split_scaled(vec, draw[j], prof[w, j, 1:2, :], j)
        sums = [None] * blocks
        for t, (i, j) in enumerate(tile_pairs(blocks)):
            multiply(sums, vec, kern[0, t], i, j)
        sums = joined(sums, lambda j: prof[w, j, 1:2, :], samples)
        keep_pieces(stage, w, sums, pieces, width)

    @pl.when(w == own)
    def _():
        close_all(own, batch, copies_in, copies_out)
        out[...] = landed[...]


def own_bins(label, at, start, samples):
    return jnp.broadcast_to(label[:, at], (samples, CHUNK)) - start


def field_group(samples, rows, data, own, pair):
    part = jnp.concatenate([rows[pair + i] for i in range(GROUP // 2)], axis=0)
    full = dot(part, data, NT)
    total = jnp.zeros((samples, CHUNK), jnp.float32)
    for b in range(GROUP):
        total = total + jnp.where(own == b, full[b * samples : (b + 1) * samples, :], 0.0)
    return total


def sums_group(value, data, own):
    full = jnp.concatenate([jnp.where(own == b, value, 0.0) for b in range(GROUP)], axis=0)
    return dot(full.astype(jnp.bfloat16), data, NN)


def chunk_at(c):
    return pl.ds(pl.multiple_of(c * CHUNK, CHUNK), CHUNK)


def fetch(basis, c, held, sem):
    copy = pltpu.make_async_copy(basis.at[chunk_at(c)], held, sem)
    copy.start()
    copy.wait()


def rest_field_kernel(samples, chunks, bins, rows, label, basis, extra, pairs, trips, held, sem):
    extra[...] = jnp.zeros_like(extra)

    def over(c, _):
        pair = bins[0, c * CHUNK] // 2
        start = pair * 2
        count = (bins[0, c * CHUNK + CHUNK - 1] - start) // GROUP + 1
        pairs[c] = pair
        trips[c] = count

        @pl.when(count > 1)
        def _():
            fetch(basis, c, held, sem)

            def more(k, total):
                first = start + k * GROUP
                own = own_bins(label, chunk_at(c), first, samples)
                return total + field_group(samples, rows, held[...], own, first // 2)

            extra[c] = lax.fori_loop(1, count, more, jnp.zeros((samples, CHUNK), jnp.float32))

        return 0

    lax.fori_loop(0, chunks, over, 0)


def rest_sums_kernel(samples, chunks, halves, per, pairs, trips, terms, weight, label, basis, sums, held, sem):
    sums[...] = jnp.zeros_like(sums)

    def put(start, term):
        sums[pl.ds(pl.multiple_of(start * samples, 2 * samples), GROUP * samples), :] += term

    def over(c, _):
        start, count = pairs[c] * 2, trips[c]
        put(start, terms[c])

        @pl.when(count > 1)
        def _():
            fetch(basis, c, held, sem)
            part, at = c // per, chunk_at(c % per)
            value = weight[part // halves, part % halves, :, at].astype(jnp.float32)

            def more(k, _):
                first = start + k * GROUP
                own = own_bins(label, chunk_at(c), first, samples)
                put(first, sums_group(value, held[...], own))
                return 0

            lax.fori_loop(1, count, more, 0)

        return 0

    lax.fori_loop(0, chunks, over, 0)


def events_kernel(
    axis, count, samples, halves, per,
    pairs, rows, label, extra, basis, terms, weight,
    held, partial, landed, send, recv, load,
):
    me = lax.axis_index(axis)
    parts = count * halves
    size = per * CHUNK

    def place(n):
        return lax.rem(me + 1 + lax.rem(n, count), count), n // count

    def loading(n):
        p, h = place(n)
        at = pl.ds(pl.multiple_of((p * halves + h) * size, size), size)
        return pltpu.make_async_copy(basis.at[at], held.at[at], load.at[n])

    def reducing(h, d):
        p = lax.rem(me + 1 + d, count)
        return remote(axis, p, partial.at[p, h], landed.at[d, h], send.at[0, h, d], recv.at[0, h, d])

    def sharing(h, d):
        p = lax.rem(me + 1 + d, count)
        return remote(axis, p, weight.at[me, h], weight.at[me, h], send.at[1, h, d], recv.at[1, h, d])

    def begin(n, _):
        loading(n).start()
        return 0

    lax.fori_loop(0, parts, begin, 0)
    greet(axis, count)

    def field(n, _):
        p, h = place(n)
        loading(n).wait()
        for k in range(per):
            c = (p * halves + h) * per + k
            pair = pairs[c]
            own = own_bins(label, chunk_at(c), pair * 2, samples)
            total = extra[c] + field_group(samples, rows, held[chunk_at(c), :], own, pair)
            partial[p, h, :, k * CHUNK : (k + 1) * CHUNK] = total.astype(partial.dtype)

        @pl.when(lax.rem(n, count) < count - 1)
        def _():
            reducing(h, lax.rem(n, count)).start()

        return 0

    def sums(p, h):
        for k in range(per):
            c = (p * halves + h) * per + k
            own = own_bins(label, chunk_at(c), pairs[c] * 2, samples)
            value = weight[p, h, :, k * CHUNK : (k + 1) * CHUNK].astype(jnp.float32)
            terms[c] = sums_group(value, held[chunk_at(c), :], own)

    lax.fori_loop(0, parts, field, 0)

    def first(h, _):
        for d in range(count - 1):
            reducing(h, d).wait_recv()
        for k in range(per):
            at = slice(k * CHUNK, (k + 1) * CHUNK)
            total = partial[me, h, :, at].astype(jnp.float32)
            for d in range(count - 1):
                total = total + landed[d, h, :, at].astype(jnp.float32)
            weight[me, h, :, at] = (-2.0 * total / (1.0 + total * total) / samples).astype(weight.dtype)
        for d in range(count - 1):
            sharing(h, d).start()
        sums(me, h)
        return 0

    lax.fori_loop(0, halves, first, 0)

    def second(n, _):
        h, d = n // (count - 1), lax.rem(n, count - 1)
        sharing(h, d).wait_recv()
        sums(lax.rem(me + count - 1 - d, count), h)
        return 0

    lax.fori_loop(0, halves * (count - 1), second, 0)
    for h in range(halves):
        for d in range(count - 1):
            reducing(h, d).wait_send()
            sharing(h, d).wait_send()


def greet(axis, count):
    me = lax.axis_index(axis)
    peers = [lax.rem(me + d, count) for d in range(1, count)]
    barrier = pltpu.get_barrier_semaphore()
    for peer in peers:
        pl.semaphore_signal(barrier, inc=1, device_id={axis: peer}, device_id_type=MESH)
    pl.semaphore_wait(barrier, count - 1)
    return me, peers


def params(**more):
    return pltpu.CompilerParams(
        dimension_semantics=("arbitrary",), vmem_limit_bytes=60 << 20, **more
    )


def shards(count, splits, latent, basis, event_bin, length, amplitude_scale, yield_norm, bin_coords):
    samples, waves, width = latent.shape
    total = bin_coords.shape[1]
    own = waves // count
    blocks = total // TILE
    tiles = blocks * (blocks + 1) // 2
    f32, bf16 = jnp.float32, jnp.bfloat16

    profile = jnp.stack(
        [length * length, amplitude_scale * jnp.sqrt(math.sqrt(2.0) * length)], axis=1
    ).reshape(count, own, 2, width)
    draws = jnp.transpose(latent, (1, 0, 2)).reshape(count, own, samples, width)

    batch = math.gcd(own, BATCHES)
    vmem = pl.BlockSpec(memory_space=pltpu.VMEM)
    piece = jax.ShapeDtypeStruct((count, own, samples, width), bf16)
    kern_spec = pl.BlockSpec((1, tiles, TILE, TILE), lambda w: (jnp.minimum(w, own - 1), 0, 0, 0))
    stages = [
        pltpu.VMEM((own, count, samples, width), bf16),
        pltpu.VMEM((count, own, samples, width), bf16),
    ]

    def semaphores(arrays):
        return [pltpu.SemaphoreType.DMA((arrays, batch, count - 1))] * 2 + [
            pltpu.SemaphoreType.DMA((own, count - 1))
        ] * 2

    kern, amp, kept = pl.pallas_call(
        functools.partial(forward_kernel, "event", count, width, own, batch),
        out_shape=(
            jax.ShapeDtypeStruct((own, tiles, TILE, TILE), bf16),
            piece,
            jax.ShapeDtypeStruct((own, blocks, 2, TILE), f32),
        ),
        grid=(own + 1,),
        in_specs=[vmem, vmem, vmem],
        out_specs=(kern_spec, vmem, vmem),
        scratch_shapes=[
            pltpu.VMEM((tiles, TILE, TILE), f32),
            pltpu.VMEM((total, LANES), f32),
            pltpu.VMEM((total, LANES), f32),
            pltpu.VMEM((blocks, 2, TILE), f32),
            pltpu.VMEM((blocks, 2, TILE), f32),
            pltpu.VMEM((blocks, samples, TILE), bf16),
            pltpu.VMEM((blocks, 2 * samples, TILE), bf16),
            pltpu.VMEM((count, own, 2, width), f32),
            pltpu.VMEM((count, own, samples, width), bf16),
        ]
        + stages
        + semaphores(2),
        compiler_params=params(collective_id=0, has_side_effects=True),
        name="kern_forward",
    )(bin_coords, profile, draws)

    amp = amp.reshape(waves, samples, width)
    amp_rows = jnp.transpose(amp, (2, 1, 0)).reshape(width * samples, waves)
    amp_rows = jnp.pad(amp_rows, ((0, GROUP * samples), (0, 0))).reshape(-1, 2 * samples, waves)

    events = basis.shape[0]
    chunks = events // CHUNK
    halves = math.gcd(chunks // splits, HALVES)
    per = chunks // splits // halves
    smem = pl.BlockSpec(memory_space=pltpu.SMEM)
    anywhere = pl.BlockSpec(memory_space=pltpu.HBM)
    one = [pltpu.VMEM((CHUNK, waves), bf16), pltpu.SemaphoreType.DMA]
    marks = jax.ShapeDtypeStruct((chunks,), jnp.int32)
    extra, pairs, trips = pl.pallas_call(
        functools.partial(rest_field_kernel, samples, chunks),
        out_shape=(jax.ShapeDtypeStruct((chunks, samples, CHUNK), f32), marks, marks),
        in_specs=[smem, vmem, vmem, anywhere],
        out_specs=(vmem, smem, smem),
        scratch_shapes=one,
        compiler_params=pltpu.CompilerParams(vmem_limit_bytes=24 << 20),
        name="rest_field",
    )(event_bin, amp_rows, event_bin, basis)
    shared = (splits, halves, samples, per * CHUNK)
    terms, weight = pl.pallas_call(
        functools.partial(events_kernel, "wave", splits, samples, halves, per),
        out_shape=(
            jax.ShapeDtypeStruct((chunks, GROUP * samples, waves), f32),
            jax.ShapeDtypeStruct(shared, bf16),
        ),
        in_specs=[smem, vmem, vmem, vmem, anywhere],
        out_specs=(vmem, vmem),
        scratch_shapes=[
            pltpu.VMEM((events, waves), bf16),
            pltpu.VMEM(shared, bf16),
            pltpu.VMEM((splits - 1,) + shared[1:], bf16),
            pltpu.SemaphoreType.DMA((2, halves, splits - 1)),
            pltpu.SemaphoreType.DMA((2, halves, splits - 1)),
            pltpu.SemaphoreType.DMA((splits * halves,)),
        ],
        compiler_params=pltpu.CompilerParams(
            collective_id=2, has_side_effects=True, vmem_limit_bytes=40 << 20
        ),
        name="events",
    )(pairs, amp_rows, event_bin, extra, basis)
    sums = pl.pallas_call(
        functools.partial(rest_sums_kernel, samples, chunks, halves, per),
        out_shape=jax.ShapeDtypeStruct(((width + GROUP) * samples, waves), f32),
        in_specs=[smem, smem, vmem, vmem, vmem, anywhere],
        out_specs=vmem,
        scratch_shapes=one,
        compiler_params=pltpu.CompilerParams(vmem_limit_bytes=24 << 20),
        name="rest_sums",
    )(pairs, trips, terms, weight, event_bin, basis)

    sums = jnp.transpose(sums[: width * samples].reshape(width, samples, waves), (2, 1, 0))
    grad = (sums + 2.0 / samples * amp.astype(f32) * yield_norm[:, None, :]).astype(bf16)
    pulled = pl.pallas_call(
        functools.partial(backward_kernel, "event", count, width, own, batch),
        out_shape=piece,
        grid=(own + 1,),
        in_specs=[kern_spec, vmem, vmem],
        out_specs=vmem,
        scratch_shapes=[
            pltpu.VMEM((blocks, samples, TILE), bf16),
            pltpu.VMEM((blocks, 2 * samples, TILE), bf16),
            pltpu.VMEM((count, own, samples, width), bf16),
        ]
        + stages
        + semaphores(1),
        compiler_params=params(collective_id=1, has_side_effects=True),
        name="kern_backward",
    )(kern, grad.reshape(count, own, samples, width), kept)
    pulled = pulled.reshape(waves, samples, width).astype(f32)
    return jnp.transpose(pulled, (1, 0, 2)) + latent.astype(f32)


def solution(mesh):
    placed = (
        P(None, "wave", "event"),
        P("event", "wave"),
        P("event", None),
        P("wave", "event"),
        P("wave", "event"),
        P("wave", "event"),
        P(),
    )
    return jax.shard_map(
        functools.partial(shards, mesh.shape["event"], mesh.shape["wave"]),
        mesh=mesh,
        in_specs=placed,
        out_specs=P(None, "wave", "event"),
        check_vma=False,
    )
```

```python
import functools
import math

import jax
import jax.numpy as jnp
from jax import lax
from jax.experimental import pallas as pl
from jax.experimental.pallas import tpu as pltpu
from jax.sharding import PartitionSpec as P

TILE = 256
LANES = 128
CHUNK = 1024
GROUP = 16
BATCHES = 8
HALVES = 2
MESH = pl.DeviceIdType.MESH
NN = (((1,), (0,)), ((), ()))
NT = (((1,), (1,)), ((), ()))


def dot(a, b, dims):
    return lax.dot_general(a, b, dims, preferred_element_type=jnp.float32)


def spread_rows(dst, read, total):
    for k in range(total // LANES):
        row = read(k * LANES)
        dst[pl.ds(k * LANES, LANES), :] = jnp.broadcast_to(row, (LANES, LANES)).T


def gather_pieces(dst, src, pieces, width):
    for k in range(pieces):
        block, lane = (k * width) // TILE, (k * width) % TILE
        dst[block, :, lane : lane + width] = src(k)


def wide(column):
    return jnp.concatenate([column] * (TILE // LANES), axis=1)


def tile_pairs(blocks):
    return [(i, j) for i in range(blocks) for j in range(i, blocks)]


def add(held, term):
    return term if held is None else held + term


def multiply(sums, vec, tile, i, j):
    sums[j] = add(sums[j], dot(vec[i], tile, NN))
    if j > i:
        sums[i] = add(sums[i], dot(vec[j], tile, NT))


def keep_pieces(dst, slot, sums, pieces, width):
    for k in range(pieces):
        block, lane = (k * width) // TILE, (k * width) % TILE
        dst[slot, k] = sums[block][:, lane : lane + width].astype(dst.dtype)


def around(axis, count):
    me = lax.axis_index(axis)
    return me, [lax.rem(me + d, count) for d in range(1, count)]


def remote(axis, peer, src, dst, send, recv):
    return pltpu.make_async_remote_copy(
        src_ref=src,
        dst_ref=dst,
        send_sem=send,
        recv_sem=recv,
        device_id={axis: peer},
        device_id_type=MESH,
    )


def bytes_of(ref, sem):
    return pltpu.make_async_copy(ref, ref, sem)


def inward(axis, count, batch, sources, targets, send, recv):
    me, peers = around(axis, count)
    size = sources[0].shape[1] // batch

    def begin(q):
        at = pl.ds(q * size, size)
        for peer in peers:
            for a, (src, dst) in enumerate(zip(sources, targets)):
                remote(axis, peer, src.at[peer, at], dst.at[me, at], send.at[a], recv.at[a, q]).start()

    def arrive(q):
        for a, dst in enumerate(targets):
            bytes_of(dst.at[pl.ds(0, count - 1), pl.ds(q * size, size)], recv.at[a, q]).wait()

    def sent():
        for a, src in enumerate(sources):
            bytes_of(src.at[pl.ds(0, count - 1)], send.at[a]).wait()

    return begin, arrive, sent


def outward(axis, count, stage, landed, send, recv):
    me, peers = around(axis, count)

    def begin(w):
        for peer in peers:
            remote(axis, peer, stage.at[w, peer], landed.at[me, w], send, recv).start()
        landed[me, w] = stage[w, me]

    def done():
        whole = landed.at[pl.ds(0, count - 1)]
        bytes_of(whole, send).wait()
        bytes_of(whole, recv).wait()

    return begin, done


def open_batches(axis, count, batch, sources, targets, begin):
    me, _ = greet(axis, count)
    for q in range(batch):
        begin(q)
    for src, dst in zip(sources, targets):
        dst[me] = src[me]


def split_scaled(vec, value, scale, at):
    whole = value.astype(jnp.float32) * scale
    high = whole.astype(vec.dtype)
    low = (whole - high.astype(jnp.float32)).astype(vec.dtype)
    vec[at] = jnp.concatenate([high, low], axis=0)


def joined(sums, scale, samples):
    return [
        (part[:samples] + part[samples:]) * scale(block) for block, part in enumerate(sums)
    ]


def forward_kernel(
    axis, pieces, width, own, batch,
    coords, profile, latent, label, kern, amp, kept, pairs, trips,
    dist, col_x, col_y, prof, later, draw, vec, prof_all, draws_all, stage, landed,
    in_send, in_recv, out_send, out_recv, bins, mark,
):
    total = pieces * width
    blocks = total // TILE
    samples = latent.shape[2]
    step = 64
    per = own // batch
    w = pl.program_id(0)
    sources, targets = (profile, latent), (prof_all, draws_all)
    begin_in, arrive_in, sent_in = inward(axis, pieces, batch, sources, targets, in_send, in_recv)
    begin_out, done_out = outward(axis, pieces, stage, landed, out_send, out_recv)

    marking = pltpu.make_async_copy(label, bins, mark)

    def read_marks():
        marking.wait()

        def over(c, _):
            pair = lax.shift_right_logical(bins[0, c * CHUNK], 1)
            pairs[c] = pair
            trips[c] = (bins[0, c * CHUNK + CHUNK - 1] - pair * 2) // GROUP + 1
            return 0

        lax.fori_loop(0, pairs.shape[0], over, 0)

    def entries(i, j, t, r, rows, c, cols):
        own_x = col_x[pl.ds(i * TILE + r, rows), :]
        square = jnp.concatenate([own_x] * (cols // LANES), axis=1) + prof[j, 0:1, c : c + cols]
        root = lax.rsqrt(square)
        return root * jnp.exp2(dist[t, r : r + rows, c : c + cols] * (root * root))

    @pl.when(w == 0)
    def _():
        marking.start()
        open_batches(axis, pieces, batch, sources, targets, begin_in)
        spread_rows(col_x, lambda k: coords[0:1, k : k + LANES], total)
        spread_rows(col_y, lambda k: coords[1:2, k : k + LANES], total)

        def over_i(i, t0):
            def over_j(j, t):
                col = pl.ds(pl.multiple_of(j * TILE, TILE), TILE)
                x_c, y_c = coords[0:1, col], coords[1:2, col]
                for r in range(0, TILE, step):
                    row = pl.ds(pl.multiple_of(i * TILE + r, step), step)
                    dx = wide(col_x[row, :]) - x_c
                    dy = wide(col_y[row, :]) - y_c
                    dist[t, r : r + step, :] = (dx * dx + dy * dy) * (-math.log2(math.e))
                return t + 1

            return lax.fori_loop(i, blocks, over_j, t0)

        lax.fori_loop(0, blocks, over_i, 0)
        arrive_in(0)
        gather_pieces(later, lambda k: prof_all[k, 0], pieces, width)
        spread_rows(col_x, lambda k: later[k // TILE, 0:1, k % TILE : k % TILE + LANES], total)

    @pl.when(w > 0)
    def _():
        begin_out(w - 1)

    @pl.when(jnp.logical_and(w + 1 < own, lax.rem(w + 1, per) == 0))
    def _():
        arrive_in((w + 1) // per)

    @pl.when(w < own)
    def _():
        after = jnp.minimum(w + 1, own - 1)
        gather_pieces(prof, lambda k: prof_all[k, w], pieces, width)
        gather_pieces(later, lambda k: prof_all[k, after], pieces, width)
        gather_pieces(draw, lambda k: draws_all[k, w], pieces, width)
        kept[w] = prof[...]
        for j in range(blocks):
            split_scaled(vec, draw[j], prof[j, 1:2, :], j)
        sums = [None] * blocks
        for t, (i, j) in enumerate(tile_pairs(blocks)):
            if i == j:
                upper = entries(i, j, t, 0, LANES, 0, TILE)
                lower = entries(i, j, t, LANES, LANES, LANES, LANES)
                lower = jnp.concatenate([upper[:, LANES:].T, lower], axis=1)
                strips = [upper.astype(jnp.bfloat16), lower.astype(jnp.bfloat16)]
            else:
                strips = [
                    entries(i, j, t, r, step, 0, TILE).astype(jnp.bfloat16)
                    for r in range(0, TILE, step)
                ]
            tile = jnp.concatenate(strips, axis=0)
            kern[0, t] = tile
            multiply(sums, vec, tile, i, j)
            if j == blocks - 1:
                for k in range(0, TILE, LANES):
                    row = later[i, 0:1, k : k + LANES]
                    at = pl.ds(i * TILE + k, LANES)
                    col_x[at, :] = jnp.broadcast_to(row, (LANES, LANES)).T
        sums = joined(sums, lambda j: prof[j, 1:2, :], samples)
        keep_pieces(stage, w, sums, pieces, width)

    @pl.when(w == own)
    def _():
        read_marks()
        sent_in()
        done_out()
        amp[...] = landed[...]


def backward_kernel(
    axis, pieces, width, own, batch,
    kern, grad, prof, out,
    draw, vec, grad_all, stage, landed, in_send, in_recv, out_send, out_recv,
):
    total = pieces * width
    blocks = total // TILE
    samples = grad.shape[2]
    w = pl.program_id(0)
    begin_in, arrive_in, sent_in = inward(axis, pieces, batch, (grad,), (grad_all,), in_send, in_recv)
    begin_out, done_out = outward(axis, pieces, stage, landed, out_send, out_recv)

    @pl.when(w == 0)
    def _():
        open_batches(axis, pieces, batch, (grad,), (grad_all,), begin_in)

    @pl.when(w > 0)
    def _():
        begin_out(w - 1)

    @pl.when(jnp.logical_and(w < own, lax.rem(w, own // batch) == 0))
    def _():
        arrive_in(w // (own // batch))

    @pl.when(w < own)
    def _():
        gather_pieces(draw, lambda k: grad_all[k, w], pieces, width)
        for j in range(blocks):
            split_scaled(vec, draw[j], prof[w, j, 1:2, :], j)
        sums = [None] * blocks
        for t, (i, j) in enumerate(tile_pairs(blocks)):
            multiply(sums, vec, kern[0, t], i, j)
        sums = joined(sums, lambda j: prof[w, j, 1:2, :], samples)
        keep_pieces(stage, w, sums, pieces, width)

    @pl.when(w == own)
    def _():
        sent_in()
        done_out()
        out[...] = landed[...]


def own_bins(label, at, start, samples):
    return jnp.broadcast_to(label[:, at], (samples, CHUNK)) - start


def field_group(samples, rows, data, own, pair):
    part = jnp.concatenate([rows[pair + i] for i in range(GROUP // 2)], axis=0)
    full = dot(part, data, NT)
    total = jnp.zeros((samples, CHUNK), jnp.float32)
    for b in range(GROUP):
        total = total + jnp.where(own == b, full[b * samples : (b + 1) * samples, :], 0.0)
    return total


def sums_group(value, data, own):
    full = jnp.concatenate([jnp.where(own == b, value, 0.0) for b in range(GROUP)], axis=0)
    return dot(full.astype(jnp.bfloat16), data, NN)


def chunk_at(c):
    return pl.ds(pl.multiple_of(c * CHUNK, CHUNK), CHUNK)


def fetch(basis, c, held, sem):
    copy = pltpu.make_async_copy(basis.at[chunk_at(c)], held, sem)
    copy.start()
    copy.wait()


def rest_field_kernel(samples, chunks, pairs, trips, rows, label, basis, extra, held, sem):
    extra[...] = jnp.zeros_like(extra)

    def over(c, _):
        start, count = pairs[c] * 2, trips[c]

        @pl.when(count > 1)
        def _():
            fetch(basis, c, held, sem)

            def more(k, total):
                first = start + k * GROUP
                own = own_bins(label, chunk_at(c), first, samples)
                return total + field_group(samples, rows, held[...], own, first // 2)

            extra[c] = lax.fori_loop(1, count, more, jnp.zeros((samples, CHUNK), jnp.float32))

        return 0

    lax.fori_loop(0, chunks, over, 0)


def rest_sums_kernel(samples, chunks, halves, per, pairs, trips, terms, weight, label, basis, sums, held, sem):
    sums[...] = jnp.zeros_like(sums)

    def put(start, term):
        sums[pl.ds(pl.multiple_of(start * samples, 2 * samples), GROUP * samples), :] += term

    def over(c, _):
        start, count = pairs[c] * 2, trips[c]
        put(start, terms[c])

        @pl.when(count > 1)
        def _():
            fetch(basis, c, held, sem)
            part, at = c // per, chunk_at(c % per)
            value = weight[part // halves, part % halves, :, at].astype(jnp.float32)

            def more(k, _):
                first = start + k * GROUP
                own = own_bins(label, chunk_at(c), first, samples)
                put(first, sums_group(value, held[...], own))
                return 0

            lax.fori_loop(1, count, more, 0)

        return 0

    lax.fori_loop(0, chunks, over, 0)


def events_kernel(
    axis, count, samples, halves, per,
    pairs, rows, label, extra, basis, terms, weight,
    held, partial, landed, send, recv, load,
):
    me = lax.axis_index(axis)
    parts = count * halves
    size = per * CHUNK

    def place(n):
        return lax.rem(me + 1 + lax.rem(n, count), count), n // count

    def loading(n):
        p, h = place(n)
        at = pl.ds(pl.multiple_of((p * halves + h) * size, size), size)
        return pltpu.make_async_copy(basis.at[at], held.at[at], load.at[n])

    def reducing(h, d):
        p = lax.rem(me + 1 + d, count)
        return remote(axis, p, partial.at[p, h], landed.at[d, h], send.at[0, h, d], recv.at[0, h, d])

    def sharing(h, d):
        p = lax.rem(me + 1 + d, count)
        return remote(axis, p, weight.at[me, h], weight.at[me, h], send.at[1, h, d], recv.at[1, h, d])

    ahead = min(2, parts)
    for n in range(ahead):
        loading(n).start()
    greet(axis, count)

    def field(n, _):
        p, h = place(n)
        loading(n).wait()

        @pl.when(n + ahead < parts)
        def _():
            loading(n + ahead).start()

        for k in range(per):
            c = (p * halves + h) * per + k
            pair = pairs[c]
            own = own_bins(label, chunk_at(c), pair * 2, samples)
            total = extra[c] + field_group(samples, rows, held[chunk_at(c), :], own, pair)
            partial[p, h, :, k * CHUNK : (k + 1) * CHUNK] = total.astype(partial.dtype)

        @pl.when(lax.rem(n, count) < count - 1)
        def _():
            reducing(h, lax.rem(n, count)).start()

        return 0

    def sums(p, h):
        for k in range(per):
            c = (p * halves + h) * per + k
            own = own_bins(label, chunk_at(c), pairs[c] * 2, samples)
            value = weight[p, h, :, k * CHUNK : (k + 1) * CHUNK].astype(jnp.float32)
            terms[c] = sums_group(value, held[chunk_at(c), :], own)

    lax.fori_loop(0, parts, field, 0)

    def first(h, _):
        for d in range(count - 1):
            reducing(h, d).wait_recv()
        for k in range(per):
            at = slice(k * CHUNK, (k + 1) * CHUNK)
            total = partial[me, h, :, at].astype(jnp.float32)
            for d in range(count - 1):
                total = total + landed[d, h, :, at].astype(jnp.float32)
            weight[me, h, :, at] = (-2.0 * total / (1.0 + total * total) / samples).astype(weight.dtype)
        for d in range(count - 1):
            sharing(h, d).start()
        sums(me, h)
        return 0

    lax.fori_loop(0, halves, first, 0)

    def second(n, _):
        h, d = n // (count - 1), lax.rem(n, count - 1)
        sharing(h, d).wait_recv()
        sums(lax.rem(me + count - 1 - d, count), h)
        return 0

    lax.fori_loop(0, halves * (count - 1), second, 0)
    for h in range(halves):
        for d in range(count - 1):
            reducing(h, d).wait_send()
            sharing(h, d).wait_send()


def greet(axis, count):
    me = lax.axis_index(axis)
    peers = [lax.rem(me + d, count) for d in range(1, count)]
    barrier = pltpu.get_barrier_semaphore()
    for peer in peers:
        pl.semaphore_signal(barrier, inc=1, device_id={axis: peer}, device_id_type=MESH)
    pl.semaphore_wait(barrier, count - 1)
    return me, peers


def params(**more):
    return pltpu.CompilerParams(
        dimension_semantics=("arbitrary",), vmem_limit_bytes=60 << 20, **more
    )


def shards(count, splits, latent, basis, event_bin, length, amplitude_scale, yield_norm, bin_coords):
    samples, waves, width = latent.shape
    total = bin_coords.shape[1]
    own = waves // count
    blocks = total // TILE
    tiles = blocks * (blocks + 1) // 2
    f32, bf16 = jnp.float32, jnp.bfloat16

    profile = jnp.stack(
        [length * length, amplitude_scale * jnp.sqrt(math.sqrt(2.0) * length)], axis=1
    ).reshape(count, own, 2, width)
    draws = jnp.transpose(latent, (1, 0, 2)).reshape(count, own, samples, width)

    batch = math.gcd(own, BATCHES)
    vmem = pl.BlockSpec(memory_space=pltpu.VMEM)
    piece = jax.ShapeDtypeStruct((count, own, samples, width), bf16)
    kern_spec = pl.BlockSpec((1, tiles, TILE, TILE), lambda w: (jnp.minimum(w, own - 1), 0, 0, 0))
    stages = [
        pltpu.VMEM((own, count, samples, width), bf16),
        pltpu.VMEM((count, own, samples, width), bf16),
    ]

    def semaphores(arrays):
        return [
            pltpu.SemaphoreType.DMA((arrays,)),
            pltpu.SemaphoreType.DMA((arrays, batch)),
            pltpu.SemaphoreType.DMA,
            pltpu.SemaphoreType.DMA,
        ]

    events = basis.shape[0]
    chunks = events // CHUNK
    smem = pl.BlockSpec(memory_space=pltpu.SMEM)
    anywhere = pl.BlockSpec(memory_space=pltpu.HBM)
    marks = jax.ShapeDtypeStruct((chunks,), jnp.int32)
    kern, amp, kept, pairs, trips = pl.pallas_call(
        functools.partial(forward_kernel, "event", count, width, own, batch),
        out_shape=(
            jax.ShapeDtypeStruct((own, tiles, TILE, TILE), bf16),
            piece,
            jax.ShapeDtypeStruct((own, blocks, 2, TILE), f32),
            marks,
            marks,
        ),
        grid=(own + 1,),
        in_specs=[vmem, vmem, vmem, anywhere],
        out_specs=(kern_spec, vmem, vmem, smem, smem),
        scratch_shapes=[
            pltpu.VMEM((tiles, TILE, TILE), f32),
            pltpu.VMEM((total, LANES), f32),
            pltpu.VMEM((total, LANES), f32),
            pltpu.VMEM((blocks, 2, TILE), f32),
            pltpu.VMEM((blocks, 2, TILE), f32),
            pltpu.VMEM((blocks, samples, TILE), bf16),
            pltpu.VMEM((blocks, 2 * samples, TILE), bf16),
            pltpu.VMEM((count, own, 2, width), f32),
            pltpu.VMEM((count, own, samples, width), bf16),
        ]
        + stages
        + semaphores(2)
        + [pltpu.SMEM(event_bin.shape, jnp.int32), pltpu.SemaphoreType.DMA],
        compiler_params=params(collective_id=0, has_side_effects=True),
        name="kern_forward",
    )(bin_coords, profile, draws, event_bin)

    amp = amp.reshape(waves, samples, width)
    amp_rows = jnp.transpose(amp, (2, 1, 0)).reshape(width * samples, waves)
    amp_rows = jnp.pad(amp_rows, ((0, GROUP * samples), (0, 0))).reshape(-1, 2 * samples, waves)

    halves = math.gcd(chunks // splits, HALVES)
    per = chunks // splits // halves
    one = [pltpu.VMEM((CHUNK, waves), bf16), pltpu.SemaphoreType.DMA]
    extra = pl.pallas_call(
        functools.partial(rest_field_kernel, samples, chunks),
        out_shape=jax.ShapeDtypeStruct((chunks, samples, CHUNK), f32),
        in_specs=[smem, smem, vmem, vmem, anywhere],
        out_specs=vmem,
        scratch_shapes=one,
        compiler_params=pltpu.CompilerParams(vmem_limit_bytes=24 << 20),
        name="rest_field",
    )(pairs, trips, amp_rows, event_bin, basis)
    shared = (splits, halves, samples, per * CHUNK)
    terms, weight = pl.pallas_call(
        functools.partial(events_kernel, "wave", splits, samples, halves, per),
        out_shape=(
            jax.ShapeDtypeStruct((chunks, GROUP * samples, waves), f32),
            jax.ShapeDtypeStruct(shared, bf16),
        ),
        in_specs=[smem, vmem, vmem, vmem, anywhere],
        out_specs=(vmem, vmem),
        scratch_shapes=[
            pltpu.VMEM((events, waves), bf16),
            pltpu.VMEM(shared, bf16),
            pltpu.VMEM((splits - 1,) + shared[1:], bf16),
            pltpu.SemaphoreType.DMA((2, halves, splits - 1)),
            pltpu.SemaphoreType.DMA((2, halves, splits - 1)),
            pltpu.SemaphoreType.DMA((splits * halves,)),
        ],
        compiler_params=pltpu.CompilerParams(
            collective_id=2, has_side_effects=True, vmem_limit_bytes=40 << 20
        ),
        name="events",
    )(pairs, amp_rows, event_bin, extra, basis)
    sums = pl.pallas_call(
        functools.partial(rest_sums_kernel, samples, chunks, halves, per),
        out_shape=jax.ShapeDtypeStruct(((width + GROUP) * samples, waves), f32),
        in_specs=[smem, smem, vmem, vmem, vmem, anywhere],
        out_specs=vmem,
        scratch_shapes=one,
        compiler_params=pltpu.CompilerParams(vmem_limit_bytes=24 << 20),
        name="rest_sums",
    )(pairs, trips, terms, weight, event_bin, basis)

    sums = jnp.transpose(sums[: width * samples].reshape(width, samples, waves), (2, 1, 0))
    grad = (sums + 2.0 / samples * amp.astype(f32) * yield_norm[:, None, :]).astype(bf16)
    pulled = pl.pallas_call(
        functools.partial(backward_kernel, "event", count, width, own, batch),
        out_shape=piece,
        grid=(own + 1,),
        in_specs=[kern_spec, vmem, vmem],
        out_specs=vmem,
        scratch_shapes=[
            pltpu.VMEM((blocks, samples, TILE), bf16),
            pltpu.VMEM((blocks, 2 * samples, TILE), bf16),
            pltpu.VMEM((count, own, samples, width), bf16),
        ]
        + stages
        + semaphores(1),
        compiler_params=params(collective_id=1, has_side_effects=True),
        name="kern_backward",
    )(kern, grad.reshape(count, own, samples, width), kept)
    pulled = pulled.reshape(waves, samples, width).astype(f32)
    return jnp.transpose(pulled, (1, 0, 2)) + latent.astype(f32)


def solution(mesh):
    placed = (
        P(None, "wave", "event"),
        P("event", "wave"),
        P("event", None),
        P("wave", "event"),
        P("wave", "event"),
        P("wave", "event"),
        P(),
    )
    return jax.shard_map(
        functools.partial(shards, mesh.shape["event"], mesh.shape["wave"]),
        mesh=mesh,
        in_specs=placed,
        out_specs=P(None, "wave", "event"),
        check_vma=False,
    )
```

```python
import functools
import math

import jax
import jax.numpy as jnp
from jax import lax
from jax.experimental import pallas as pl
from jax.experimental.pallas import tpu as pltpu
from jax.sharding import PartitionSpec as P

TILE = 256
LANES = 128
CHUNK = 1024
GROUP = 16
BATCHES = 8
HALVES = 2
MESH = pl.DeviceIdType.MESH
NN = (((1,), (0,)), ((), ()))
NT = (((1,), (1,)), ((), ()))


def dot(a, b, dims):
    return lax.dot_general(a, b, dims, preferred_element_type=jnp.float32)


def spread_rows(dst, read, total):
    for k in range(total // LANES):
        row = read(k * LANES)
        dst[pl.ds(k * LANES, LANES), :] = jnp.broadcast_to(row, (LANES, LANES)).T


def gather_pieces(dst, src, pieces, width):
    for k in range(pieces):
        block, lane = (k * width) // TILE, (k * width) % TILE
        dst[block, :, lane : lane + width] = src(k)


def wide(column):
    return jnp.concatenate([column] * (TILE // LANES), axis=1)


def tile_pairs(blocks):
    return [(i, j) for i in range(blocks) for j in range(i, blocks)]


def add(held, term):
    return term if held is None else held + term


def multiply(sums, vec, tile, i, j):
    sums[j] = add(sums[j], dot(vec[i], tile, NN))
    if j > i:
        sums[i] = add(sums[i], dot(vec[j], tile, NT))


def keep_pieces(dst, slot, sums, pieces, width):
    for k in range(pieces):
        block, lane = (k * width) // TILE, (k * width) % TILE
        dst[slot, k] = sums[block][:, lane : lane + width].astype(dst.dtype)


def around(axis, count):
    me = lax.axis_index(axis)
    return me, [lax.rem(me + d, count) for d in range(1, count)]


def remote(axis, peer, src, dst, send, recv):
    return pltpu.make_async_remote_copy(
        src_ref=src,
        dst_ref=dst,
        send_sem=send,
        recv_sem=recv,
        device_id={axis: peer},
        device_id_type=MESH,
    )


def bytes_of(ref, sem):
    return pltpu.make_async_copy(ref, ref, sem)


def inward(axis, count, batch, sources, targets, send, recv):
    me, peers = around(axis, count)
    size = sources[0].shape[1] // batch

    def begin(q):
        at = pl.ds(q * size, size)
        for peer in peers:
            for a, (src, dst) in enumerate(zip(sources, targets)):
                remote(axis, peer, src.at[peer, at], dst.at[me, at], send.at[a], recv.at[a, q]).start()

    def arrive(q):
        for a, dst in enumerate(targets):
            bytes_of(dst.at[pl.ds(0, count - 1), pl.ds(q * size, size)], recv.at[a, q]).wait()

    def sent():
        for a, src in enumerate(sources):
            bytes_of(src.at[pl.ds(0, count - 1)], send.at[a]).wait()

    return begin, arrive, sent


def outward(axis, count, stage, landed, send, recv):
    me, peers = around(axis, count)

    def begin(w):
        for peer in peers:
            remote(axis, peer, stage.at[w, peer], landed.at[me, w], send, recv).start()
        landed[me, w] = stage[w, me]

    def done():
        whole = landed.at[pl.ds(0, count - 1)]
        bytes_of(whole, send).wait()
        bytes_of(whole, recv).wait()

    return begin, done


def open_batches(axis, count, batch, sources, targets, begin):
    me, _ = greet(axis, count)
    for q in range(batch):
        begin(q)
    for src, dst in zip(sources, targets):
        dst[me] = src[me]


def split_scaled(vec, value, scale, at):
    whole = value.astype(jnp.float32) * scale
    high = whole.astype(vec.dtype)
    low = (whole - high.astype(jnp.float32)).astype(vec.dtype)
    vec[at] = jnp.concatenate([high, low], axis=0)


def joined(sums, scale, samples):
    return [
        (part[:samples] + part[samples:]) * scale(block) for block, part in enumerate(sums)
    ]


def forward_kernel(
    axis, pieces, width, own, batch,
    coords, profile, latent, label, kern, amp, kept, pairs, trips,
    dist, col_x, col_y, prof, later, draw, vec, prof_all, draws_all, stage, landed,
    in_send, in_recv, out_send, out_recv, bins, mark,
):
    total = pieces * width
    blocks = total // TILE
    samples = latent.shape[2]
    step = 64
    per = own // batch
    w = pl.program_id(0)
    sources, targets = (profile, latent), (prof_all, draws_all)
    begin_in, arrive_in, sent_in = inward(axis, pieces, batch, sources, targets, in_send, in_recv)
    begin_out, done_out = outward(axis, pieces, stage, landed, out_send, out_recv)

    marking = pltpu.make_async_copy(label, bins, mark)

    def read_marks():
        marking.wait()

        def over(c, _):
            pair = lax.shift_right_logical(bins[0, c * CHUNK], 1)
            pairs[c] = pair
            trips[c] = (bins[0, c * CHUNK + CHUNK - 1] - pair * 2) // GROUP + 1
            return 0

        lax.fori_loop(0, pairs.shape[0], over, 0)

    def entries(i, j, t, r, rows, c, cols):
        own_x = col_x[pl.ds(i * TILE + r, rows), :]
        square = jnp.concatenate([own_x] * (cols // LANES), axis=1) + prof[j, 0:1, c : c + cols]
        root = lax.rsqrt(square)
        return root * jnp.exp2(dist[t, r : r + rows, c : c + cols] * (root * root))

    @pl.when(w == 0)
    def _():
        marking.start()
        open_batches(axis, pieces, batch, sources, targets, begin_in)
        spread_rows(col_x, lambda k: coords[0:1, k : k + LANES], total)
        spread_rows(col_y, lambda k: coords[1:2, k : k + LANES], total)

        def over_i(i, t0):
            def over_j(j, t):
                col = pl.ds(pl.multiple_of(j * TILE, TILE), TILE)
                x_c, y_c = coords[0:1, col], coords[1:2, col]
                for r in range(0, TILE, step):
                    row = pl.ds(pl.multiple_of(i * TILE + r, step), step)
                    dx = wide(col_x[row, :]) - x_c
                    dy = wide(col_y[row, :]) - y_c
                    dist[t, r : r + step, :] = (dx * dx + dy * dy) * (-math.log2(math.e))
                return t + 1

            return lax.fori_loop(i, blocks, over_j, t0)

        lax.fori_loop(0, blocks, over_i, 0)
        arrive_in(0)
        gather_pieces(later, lambda k: prof_all[k, 0], pieces, width)
        spread_rows(col_x, lambda k: later[k // TILE, 0:1, k % TILE : k % TILE + LANES], total)

    @pl.when(w > 0)
    def _():
        begin_out(w - 1)

    @pl.when(jnp.logical_and(w + 1 < own, lax.rem(w + 1, per) == 0))
    def _():
        arrive_in((w + 1) // per)

    @pl.when(w < own)
    def _():
        after = jnp.minimum(w + 1, own - 1)
        gather_pieces(prof, lambda k: prof_all[k, w], pieces, width)
        gather_pieces(later, lambda k: prof_all[k, after], pieces, width)
        gather_pieces(draw, lambda k: draws_all[k, w], pieces, width)
        kept[w] = prof[...]
        for j in range(blocks):
            split_scaled(vec, draw[j], prof[j, 1:2, :], j)
        sums = [None] * blocks
        for t, (i, j) in sorted(enumerate(tile_pairs(blocks)), key=lambda p: (-p[1][0], p[1][1])):
            if i == j:
                upper = entries(i, j, t, 0, LANES, 0, TILE)
                lower = entries(i, j, t, LANES, LANES, LANES, LANES)
                lower = jnp.concatenate([upper[:, LANES:].T, lower], axis=1)
                strips = [upper.astype(jnp.bfloat16), lower.astype(jnp.bfloat16)]
            else:
                strips = [
                    entries(i, j, t, r, step, 0, TILE).astype(jnp.bfloat16)
                    for r in range(0, TILE, step)
                ]
            tile = jnp.concatenate(strips, axis=0)
            kern[0, t] = tile
            multiply(sums, vec, tile, i, j)
            if j == blocks - 1:
                for k in range(0, TILE, LANES):
                    row = later[i, 0:1, k : k + LANES]
                    at = pl.ds(i * TILE + k, LANES)
                    col_x[at, :] = jnp.broadcast_to(row, (LANES, LANES)).T
        sums = joined(sums, lambda j: prof[j, 1:2, :], samples)
        keep_pieces(stage, w, sums, pieces, width)

    @pl.when(w == own)
    def _():
        read_marks()
        sent_in()
        done_out()
        amp[...] = landed[...]


def backward_kernel(
    axis, pieces, width, own, batch,
    kern, grad, prof, out,
    draw, vec, grad_all, stage, landed, in_send, in_recv, out_send, out_recv,
):
    total = pieces * width
    blocks = total // TILE
    samples = grad.shape[2]
    w = pl.program_id(0)
    begin_in, arrive_in, sent_in = inward(axis, pieces, batch, (grad,), (grad_all,), in_send, in_recv)
    begin_out, done_out = outward(axis, pieces, stage, landed, out_send, out_recv)

    @pl.when(w == 0)
    def _():
        open_batches(axis, pieces, batch, (grad,), (grad_all,), begin_in)

    @pl.when(w > 0)
    def _():
        begin_out(w - 1)

    @pl.when(jnp.logical_and(w < own, lax.rem(w, own // batch) == 0))
    def _():
        arrive_in(w // (own // batch))

    @pl.when(w < own)
    def _():
        gather_pieces(draw, lambda k: grad_all[k, w], pieces, width)
        for j in range(blocks):
            split_scaled(vec, draw[j], prof[w, j, 1:2, :], j)
        sums = [None] * blocks
        for t, (i, j) in enumerate(tile_pairs(blocks)):
            multiply(sums, vec, kern[0, t], i, j)
        sums = joined(sums, lambda j: prof[w, j, 1:2, :], samples)
        keep_pieces(stage, w, sums, pieces, width)

    @pl.when(w == own)
    def _():
        sent_in()
        done_out()
        out[...] = landed[...]


def own_bins(label, at, start, samples):
    return jnp.broadcast_to(label[:, at], (samples, CHUNK)) - start


def field_group(samples, rows, data, own, pair):
    part = jnp.concatenate([rows[pair + i] for i in range(GROUP // 2)], axis=0)
    full = dot(part, data, NT)
    total = jnp.zeros((samples, CHUNK), jnp.float32)
    for b in range(GROUP):
        total = total + jnp.where(own == b, full[b * samples : (b + 1) * samples, :], 0.0)
    return total


def sums_group(value, data, own):
    full = jnp.concatenate([jnp.where(own == b, value, 0.0) for b in range(GROUP)], axis=0)
    return dot(full.astype(jnp.bfloat16), data, NN)


def chunk_at(c):
    return pl.ds(pl.multiple_of(c * CHUNK, CHUNK), CHUNK)


def fetch(basis, c, held, sem):
    copy = pltpu.make_async_copy(basis.at[chunk_at(c)], held, sem)
    copy.start()
    copy.wait()


def every(start, size, stride):
    return pl.ds(start, size, stride=stride)


def lane_pieces(width):
    piece = min(width, LANES)
    return [(k, slice(k * piece, (k + 1) * piece)) for k in range(width // piece)]


def filled(value):
    return jnp.concatenate([value] * (LANES // value.shape[1]), axis=1)


def spread_samples(wide_rows, source):
    waves, samples, width = source.shape
    for k, at in lane_pieces(width):
        flat = source[:, :, at].astype(jnp.float32).reshape(waves * samples, -1)
        wide_rows[k] = filled(flat)


def prepare_kernel(latent, length, amplitude_scale, draws, profile, wide_rows):
    samples, waves, width = latent.shape
    profile[:, 0, :] = length[...] * length[...]
    profile[:, 1, :] = amplitude_scale[...] * jnp.sqrt(math.sqrt(2.0) * length[...])
    for k, at in lane_pieces(width):
        for s in range(samples):
            wide_rows[k, every(s, waves, samples), :] = filled(latent[s, :, at].astype(jnp.float32))
        whole = wide_rows[k].reshape(waves, samples, LANES)
        draws[:, :, at] = whole[:, :, : min(width, LANES)].astype(draws.dtype)


def finish_kernel(pulled, latent, out, wide_rows):
    samples, waves, width = latent.shape
    spread_samples(wide_rows, pulled)
    for k, at in lane_pieces(width):
        for s in range(samples):
            value = wide_rows[k, every(s, waves, samples), :][:, : min(width, LANES)]
            out[s, :, at] = value + latent[s, :, at].astype(jnp.float32)


def rest_field_kernel(samples, chunks, pairs, trips, amp, label, basis, rows, extra, wide_rows, turned, held, sem):
    waves, _, width = amp.shape
    extra[...] = jnp.zeros_like(extra)
    spread_samples(wide_rows, amp)
    for k, at in lane_pieces(width):
        size = at.stop - at.start
        for s in range(samples):
            part = wide_rows[k, every(s, waves, samples), :].T[:size]
            turned[every(at.start * samples + s, size, samples), :] = part
    half = width // 2
    rows[:half] = turned[...].astype(rows.dtype).reshape(half, 2 * samples, waves)
    rows[half:] = jnp.zeros((GROUP // 2, 2 * samples, waves), rows.dtype)

    def over(c, _):
        start, count = pairs[c] * 2, trips[c]

        @pl.when(count > 1)
        def _():
            fetch(basis, c, held, sem)

            def more(k, total):
                first = start + k * GROUP
                own = own_bins(label, chunk_at(c), first, samples)
                return total + field_group(samples, rows, held[...], own, first // 2)

            extra[c] = lax.fori_loop(1, count, more, jnp.zeros((samples, CHUNK), jnp.float32))

        return 0

    lax.fori_loop(0, chunks, over, 0)


def rest_sums_kernel(
    samples, chunks, halves, per,
    pairs, trips, terms, weight, label, amp, yield_norm, basis, grad,
    sums, wide_rows, held, sem,
):
    waves, _, width = amp.shape
    sums[...] = jnp.zeros_like(sums)

    def put(start, term):
        sums[pl.ds(pl.multiple_of(start * samples, 2 * samples), GROUP * samples), :] += term

    def over(c, _):
        start, count = pairs[c] * 2, trips[c]
        put(start, terms[c])

        @pl.when(count > 1)
        def _():
            fetch(basis, c, held, sem)
            part, at = c // per, chunk_at(c % per)
            value = weight[part // halves, part % halves, :, at].astype(jnp.float32)

            def more(k, _):
                first = start + k * GROUP
                own = own_bins(label, chunk_at(c), first, samples)
                put(first, sums_group(value, held[...], own))
                return 0

            lax.fori_loop(1, count, more, 0)

        return 0

    lax.fori_loop(0, chunks, over, 0)
    spread_samples(wide_rows, amp)
    for k, at in lane_pieces(width):
        size = at.stop - at.start
        norm = filled(yield_norm[:, at]) * (2.0 / samples)
        for s in range(samples):
            mine = every(s, waves, samples)
            part = sums[every(at.start * samples + s, size, samples), :]
            part = jnp.concatenate([part] * (LANES // size), axis=0).T
            wide_rows[k, mine, :] = part + wide_rows[k, mine, :] * norm
        whole = wide_rows[k].reshape(waves, samples, LANES)
        grad[:, :, at] = whole[:, :, :size].astype(grad.dtype)


def events_kernel(
    axis, count, samples, halves, per,
    pairs, rows, label, extra, basis, terms, weight,
    held, partial, landed, send, recv, load,
):
    me = lax.axis_index(axis)
    parts = count * halves
    size = per * CHUNK

    def place(n):
        return lax.rem(me + 1 + lax.rem(n, count), count), n // count

    def loading(n):
        p, h = place(n)
        at = pl.ds(pl.multiple_of((p * halves + h) * size, size), size)
        return pltpu.make_async_copy(basis.at[at], held.at[at], load.at[n])

    def reducing(h, d):
        p = lax.rem(me + 1 + d, count)
        return remote(axis, p, partial.at[p, h], landed.at[d, h], send.at[0, h, d], recv.at[0, h, d])

    def sharing(h, d):
        p = lax.rem(me + 1 + d, count)
        return remote(axis, p, weight.at[me, h], weight.at[me, h], send.at[1, h, d], recv.at[1, h, d])

    ahead = min(2, parts)
    for n in range(ahead):
        loading(n).start()
    greet(axis, count)

    def field(n, _):
        p, h = place(n)
        loading(n).wait()

        @pl.when(n + ahead < parts)
        def _():
            loading(n + ahead).start()

        for k in range(per):
            c = (p * halves + h) * per + k
            pair = pairs[c]
            own = own_bins(label, chunk_at(c), pair * 2, samples)
            total = extra[c] + field_group(samples, rows, held[chunk_at(c), :], own, pair)
            partial[p, h, :, k * CHUNK : (k + 1) * CHUNK] = total.astype(partial.dtype)

        @pl.when(lax.rem(n, count) < count - 1)
        def _():
            reducing(h, lax.rem(n, count)).start()

        return 0

    def sums(p, h):
        for k in range(per):
            c = (p * halves + h) * per + k
            own = own_bins(label, chunk_at(c), pairs[c] * 2, samples)
            value = weight[p, h, :, k * CHUNK : (k + 1) * CHUNK].astype(jnp.float32)
            terms[c] = sums_group(value, held[chunk_at(c), :], own)

    lax.fori_loop(0, parts, field, 0)

    def first(h, _):
        for d in range(count - 1):
            reducing(h, d).wait_recv()
        for k in range(per):
            at = slice(k * CHUNK, (k + 1) * CHUNK)
            total = partial[me, h, :, at].astype(jnp.float32)
            for d in range(count - 1):
                total = total + landed[d, h, :, at].astype(jnp.float32)
            weight[me, h, :, at] = (-2.0 * total / (1.0 + total * total) / samples).astype(weight.dtype)
        for d in range(count - 1):
            sharing(h, d).start()
        sums(me, h)
        return 0

    lax.fori_loop(0, halves, first, 0)

    def second(n, _):
        h, d = n // (count - 1), lax.rem(n, count - 1)
        sharing(h, d).wait_recv()
        sums(lax.rem(me + count - 1 - d, count), h)
        return 0

    lax.fori_loop(0, halves * (count - 1), second, 0)
    for h in range(halves):
        for d in range(count - 1):
            reducing(h, d).wait_send()
            sharing(h, d).wait_send()


def greet(axis, count):
    me = lax.axis_index(axis)
    peers = [lax.rem(me + d, count) for d in range(1, count)]
    barrier = pltpu.get_barrier_semaphore()
    for peer in peers:
        pl.semaphore_signal(barrier, inc=1, device_id={axis: peer}, device_id_type=MESH)
    pl.semaphore_wait(barrier, count - 1)
    return me, peers


def params(**more):
    return pltpu.CompilerParams(
        dimension_semantics=("arbitrary",), vmem_limit_bytes=60 << 20, **more
    )


def shards(count, splits, latent, basis, event_bin, length, amplitude_scale, yield_norm, bin_coords):
    samples, waves, width = latent.shape
    total = bin_coords.shape[1]
    own = waves // count
    blocks = total // TILE
    tiles = blocks * (blocks + 1) // 2
    f32, bf16 = jnp.float32, jnp.bfloat16

    sheets = pltpu.VMEM((max(width // LANES, 1), waves * samples, LANES), f32)
    turned_shape = jax.ShapeDtypeStruct((waves, samples, width), bf16)

    def local(body, name, out_shape, in_specs, out_specs, scratch_shapes):
        return pl.pallas_call(
            body,
            out_shape=out_shape,
            in_specs=in_specs,
            out_specs=out_specs,
            scratch_shapes=scratch_shapes,
            compiler_params=pltpu.CompilerParams(vmem_limit_bytes=57 << 20),
            name=name,
        )

    vmem = pl.BlockSpec(memory_space=pltpu.VMEM)
    draws, profile = local(
        prepare_kernel,
        "prepare",
        (turned_shape, jax.ShapeDtypeStruct((waves, 2, width), f32)),
        [vmem] * 3,
        (vmem, vmem),
        [sheets],
    )(latent, length, amplitude_scale)
    profile = profile.reshape(count, own, 2, width)
    draws = draws.reshape(count, own, samples, width)

    batch = math.gcd(own, BATCHES)
    piece = jax.ShapeDtypeStruct((count, own, samples, width), bf16)
    kern_spec = pl.BlockSpec((1, tiles, TILE, TILE), lambda w: (jnp.minimum(w, own - 1), 0, 0, 0))
    stages = [
        pltpu.VMEM((own, count, samples, width), bf16),
        pltpu.VMEM((count, own, samples, width), bf16),
    ]

    def semaphores(arrays):
        return [
            pltpu.SemaphoreType.DMA((arrays,)),
            pltpu.SemaphoreType.DMA((arrays, batch)),
            pltpu.SemaphoreType.DMA,
            pltpu.SemaphoreType.DMA,
        ]

    events = basis.shape[0]
    chunks = events // CHUNK
    smem = pl.BlockSpec(memory_space=pltpu.SMEM)
    anywhere = pl.BlockSpec(memory_space=pltpu.HBM)
    marks = jax.ShapeDtypeStruct((chunks,), jnp.int32)
    kern, amp, kept, pairs, trips = pl.pallas_call(
        functools.partial(forward_kernel, "event", count, width, own, batch),
        out_shape=(
            jax.ShapeDtypeStruct((own, tiles, TILE, TILE), bf16),
            piece,
            jax.ShapeDtypeStruct((own, blocks, 2, TILE), f32),
            marks,
            marks,
        ),
        grid=(own + 1,),
        in_specs=[vmem, vmem, vmem, anywhere],
        out_specs=(kern_spec, vmem, vmem, smem, smem),
        scratch_shapes=[
            pltpu.VMEM((tiles, TILE, TILE), f32),
            pltpu.VMEM((total, LANES), f32),
            pltpu.VMEM((total, LANES), f32),
            pltpu.VMEM((blocks, 2, TILE), f32),
            pltpu.VMEM((blocks, 2, TILE), f32),
            pltpu.VMEM((blocks, samples, TILE), bf16),
            pltpu.VMEM((blocks, 2 * samples, TILE), bf16),
            pltpu.VMEM((count, own, 2, width), f32),
            pltpu.VMEM((count, own, samples, width), bf16),
        ]
        + stages
        + semaphores(2)
        + [pltpu.SMEM(event_bin.shape, jnp.int32), pltpu.SemaphoreType.DMA],
        compiler_params=params(collective_id=0, has_side_effects=True),
        name="kern_forward",
    )(bin_coords, profile, draws, event_bin)

    amp = amp.reshape(waves, samples, width)
    halves = math.gcd(chunks // splits, HALVES)
    per = chunks // splits // halves
    one = [pltpu.VMEM((CHUNK, waves), bf16), pltpu.SemaphoreType.DMA]
    amp_rows, extra = local(
        functools.partial(rest_field_kernel, samples, chunks),
        "rest_field",
        (
            jax.ShapeDtypeStruct(((width + GROUP) // 2, 2 * samples, waves), bf16),
            jax.ShapeDtypeStruct((chunks, samples, CHUNK), f32),
        ),
        [smem, smem, vmem, vmem, anywhere],
        (vmem, vmem),
        [sheets, pltpu.VMEM((width * samples, waves), f32)] + one,
    )(pairs, trips, amp, event_bin, basis)
    shared = (splits, halves, samples, per * CHUNK)
    terms, weight = pl.pallas_call(
        functools.partial(events_kernel, "wave", splits, samples, halves, per),
        out_shape=(
            jax.ShapeDtypeStruct((chunks, GROUP * samples, waves), f32),
            jax.ShapeDtypeStruct(shared, bf16),
        ),
        in_specs=[smem, vmem, vmem, vmem, anywhere],
        out_specs=(vmem, vmem),
        scratch_shapes=[
            pltpu.VMEM((events, waves), bf16),
            pltpu.VMEM(shared, bf16),
            pltpu.VMEM((splits - 1,) + shared[1:], bf16),
            pltpu.SemaphoreType.DMA((2, halves, splits - 1)),
            pltpu.SemaphoreType.DMA((2, halves, splits - 1)),
            pltpu.SemaphoreType.DMA((splits * halves,)),
        ],
        compiler_params=pltpu.CompilerParams(
            collective_id=2, has_side_effects=True, vmem_limit_bytes=57 << 20
        ),
        name="events",
    )(pairs, amp_rows, event_bin, extra, basis)
    grad = local(
        functools.partial(rest_sums_kernel, samples, chunks, halves, per),
        "rest_sums",
        turned_shape,
        [smem, smem] + [vmem] * 5 + [anywhere],
        vmem,
        [pltpu.VMEM(((width + GROUP) * samples, waves), f32), sheets] + one,
    )(pairs, trips, terms, weight, event_bin, amp, yield_norm, basis)
    pulled = pl.pallas_call(
        functools.partial(backward_kernel, "event", count, width, own, batch),
        out_shape=piece,
        grid=(own + 1,),
        in_specs=[kern_spec, vmem, vmem],
        out_specs=vmem,
        scratch_shapes=[
            pltpu.VMEM((blocks, samples, TILE), bf16),
            pltpu.VMEM((blocks, 2 * samples, TILE), bf16),
            pltpu.VMEM((count, own, samples, width), bf16),
        ]
        + stages
        + semaphores(1),
        compiler_params=params(collective_id=1, has_side_effects=True),
        name="kern_backward",
    )(kern, grad.reshape(count, own, samples, width), kept)
    return local(
        finish_kernel,
        "finish",
        jax.ShapeDtypeStruct(latent.shape, f32),
        [vmem, vmem],
        vmem,
        [sheets],
    )(pulled.reshape(waves, samples, width), latent)


def solution(mesh):
    placed = (
        P(None, "wave", "event"),
        P("event", "wave"),
        P("event", None),
        P("wave", "event"),
        P("wave", "event"),
        P("wave", "event"),
        P(),
    )
    return jax.shard_map(
        functools.partial(shards, mesh.shape["event"], mesh.shape["wave"]),
        mesh=mesh,
        in_specs=placed,
        out_specs=P(None, "wave", "event"),
        check_vma=False,
    )
```

```python
import functools
import math

import jax
import jax.numpy as jnp
from jax import lax
from jax.experimental import pallas as pl
from jax.experimental.pallas import tpu as pltpu
from jax.sharding import PartitionSpec as P

TILE = 256
LANES = 128
CHUNK = 1024
GROUP = 24
BATCHES = 8
HALVES = 2
AHEAD = 8
MESH = pl.DeviceIdType.MESH
NN = (((1,), (0,)), ((), ()))
NT = (((1,), (1,)), ((), ()))


def dot(a, b, dims):
    return lax.dot_general(a, b, dims, preferred_element_type=jnp.float32)


def spread_rows(dst, read, total):
    for k in range(total // LANES):
        row = read(k * LANES)
        dst[pl.ds(k * LANES, LANES), :] = jnp.broadcast_to(row, (LANES, LANES)).T


def gather_pieces(dst, src, pieces, width):
    for k in range(pieces):
        block, lane = (k * width) // TILE, (k * width) % TILE
        dst[block, :, lane : lane + width] = src(k)


def wide(column):
    return jnp.concatenate([column] * (TILE // LANES), axis=1)


def tile_pairs(blocks):
    return [(i, j) for i in range(blocks) for j in range(i, blocks)]


def add(held, term):
    return term if held is None else held + term


def multiply(sums, vec, tile, i, j):
    sums[j] = add(sums[j], dot(vec[i], tile, NN))
    if j > i:
        sums[i] = add(sums[i], dot(vec[j], tile, NT))


def keep_pieces(dst, slot, sums, pieces, width):
    for k in range(pieces):
        block, lane = (k * width) // TILE, (k * width) % TILE
        dst[slot, k] = sums[block][:, lane : lane + width].astype(dst.dtype)


def around(axis, count):
    me = lax.axis_index(axis)
    return me, [lax.rem(me + d, count) for d in range(1, count)]


def remote(axis, peer, src, dst, send, recv):
    return pltpu.make_async_remote_copy(
        src_ref=src,
        dst_ref=dst,
        send_sem=send,
        recv_sem=recv,
        device_id={axis: peer},
        device_id_type=MESH,
    )


def bytes_of(ref, sem):
    return pltpu.make_async_copy(ref, ref, sem)


def inward(axis, count, batch, sources, targets, send, recv):
    me, peers = around(axis, count)
    size = sources[0].shape[1] // batch

    def begin(q):
        at = pl.ds(q * size, size)
        for peer in peers:
            for a, (src, dst) in enumerate(zip(sources, targets)):
                remote(axis, peer, src.at[peer, at], dst.at[me, at], send.at[a], recv.at[a, q]).start()

    def arrive(q):
        for a, dst in enumerate(targets):
            bytes_of(dst.at[pl.ds(0, count - 1), pl.ds(q * size, size)], recv.at[a, q]).wait()

    def sent():
        for a, src in enumerate(sources):
            bytes_of(src.at[pl.ds(0, count - 1)], send.at[a]).wait()

    return begin, arrive, sent


def outward(axis, count, stage, landed, send, recv):
    me, peers = around(axis, count)

    def begin(w):
        for peer in peers:
            remote(axis, peer, stage.at[w, peer], landed.at[me, w], send, recv).start()
        landed[me, w] = stage[w, me]

    def done():
        whole = landed.at[pl.ds(0, count - 1)]
        bytes_of(whole, send).wait()
        bytes_of(whole, recv).wait()

    return begin, done


def open_batches(axis, count, batch, sources, targets, begin):
    me = lax.axis_index(axis)
    hear(count)
    for q in range(batch):
        begin(q)
    for src, dst in zip(sources, targets):
        dst[me] = src[me]


def split_scaled(vec, value, scale, at):
    whole = value.astype(jnp.float32) * scale
    high = whole.astype(vec.dtype)
    low = (whole - high.astype(jnp.float32)).astype(vec.dtype)
    vec[at] = jnp.concatenate([high, low], axis=0)


def joined(sums, scale, samples):
    return [
        (part[:samples] + part[samples:]) * scale(block) for block, part in enumerate(sums)
    ]


def forward_kernel(
    axis, pieces, width, own, batch,
    coords, profile, latent, label, kern, amp, kept, pairs, trips,
    dist, col_x, col_y, prof, later, draw, vec, prof_all, draws_all, stage, landed,
    in_send, in_recv, out_send, out_recv, bins, mark,
):
    total = pieces * width
    blocks = total // TILE
    samples = latent.shape[2]
    step = 64
    per = own // batch
    w = pl.program_id(0)
    sources, targets = (profile, latent), (prof_all, draws_all)
    begin_in, arrive_in, sent_in = inward(axis, pieces, batch, sources, targets, in_send, in_recv)
    begin_out, done_out = outward(axis, pieces, stage, landed, out_send, out_recv)

    marking = pltpu.make_async_copy(label, bins, mark)

    def read_marks():
        marking.wait()

        def over(c, _):
            pair = lax.shift_right_logical(bins[0, c * CHUNK], 1)
            pairs[c] = pair
            trips[c] = (bins[0, c * CHUNK + CHUNK - 1] - pair * 2) // GROUP + 1
            return 0

        lax.fori_loop(0, pairs.shape[0], over, 0)

    def entries(i, j, t, r, rows, c, cols):
        own_x = col_x[pl.ds(i * TILE + r, rows), :]
        square = jnp.concatenate([own_x] * (cols // LANES), axis=1) + prof[j, 0:1, c : c + cols]
        root = lax.rsqrt(square)
        return root * jnp.exp2(dist[t, r : r + rows, c : c + cols] * (root * root))

    @pl.when(w == 0)
    def _():
        hail(axis, pieces)
        marking.start()
        spread_rows(col_x, lambda k: coords[0:1, k : k + LANES], total)
        spread_rows(col_y, lambda k: coords[1:2, k : k + LANES], total)
        open_batches(axis, pieces, batch, sources, targets, begin_in)

        def over_i(i, t0):
            def over_j(j, t):
                col = pl.ds(pl.multiple_of(j * TILE, TILE), TILE)
                x_c, y_c = coords[0:1, col], coords[1:2, col]
                for r in range(0, TILE, step):
                    row = pl.ds(pl.multiple_of(i * TILE + r, step), step)
                    dx = wide(col_x[row, :]) - x_c
                    dy = wide(col_y[row, :]) - y_c
                    dist[t, r : r + step, :] = (dx * dx + dy * dy) * (-math.log2(math.e))
                return t + 1

            return lax.fori_loop(i, blocks, over_j, t0)

        lax.fori_loop(0, blocks, over_i, 0)
        arrive_in(0)
        gather_pieces(later, lambda k: prof_all[k, 0], pieces, width)
        spread_rows(col_x, lambda k: later[k // TILE, 0:1, k % TILE : k % TILE + LANES], total)

    @pl.when(w > 0)
    def _():
        begin_out(w - 1)

    @pl.when(jnp.logical_and(w + 1 < own, lax.rem(w + 1, per) == 0))
    def _():
        arrive_in((w + 1) // per)

    @pl.when(w < own)
    def _():
        after = jnp.minimum(w + 1, own - 1)
        gather_pieces(prof, lambda k: prof_all[k, w], pieces, width)
        gather_pieces(later, lambda k: prof_all[k, after], pieces, width)
        gather_pieces(draw, lambda k: draws_all[k, w], pieces, width)
        kept[w] = prof[...]
        for j in range(blocks):
            split_scaled(vec, draw[j], prof[j, 1:2, :], j)
        sums = [None] * blocks
        for t, (i, j) in sorted(enumerate(tile_pairs(blocks)), key=lambda p: (-p[1][0], p[1][1])):
            if i == j:
                upper = entries(i, j, t, 0, LANES, 0, TILE)
                lower = entries(i, j, t, LANES, LANES, LANES, LANES)
                lower = jnp.concatenate([upper[:, LANES:].T, lower], axis=1)
                strips = [upper.astype(jnp.bfloat16), lower.astype(jnp.bfloat16)]
            else:
                strips = [
                    entries(i, j, t, r, step, 0, TILE).astype(jnp.bfloat16)
                    for r in range(0, TILE, step)
                ]
            tile = jnp.concatenate(strips, axis=0)
            kern[0, t] = tile
            multiply(sums, vec, tile, i, j)
            if j == blocks - 1:
                for k in range(0, TILE, LANES):
                    row = later[i, 0:1, k : k + LANES]
                    at = pl.ds(i * TILE + k, LANES)
                    col_x[at, :] = jnp.broadcast_to(row, (LANES, LANES)).T
        sums = joined(sums, lambda j: prof[j, 1:2, :], samples)
        keep_pieces(stage, w, sums, pieces, width)

    @pl.when(w == own)
    def _():
        read_marks()
        sent_in()
        done_out()
        amp[...] = landed[...]


def backward_kernel(
    axis, pieces, width, own, batch, slots,
    kern, grad, prof, out,
    tiles, turned, draw, vec, grad_all, stage, landed, load, in_send, in_recv, out_send, out_recv,
):
    total = pieces * width
    blocks = total // TILE
    samples = grad.shape[2]
    w = pl.program_id(0)
    begin_in, arrive_in, sent_in = inward(axis, pieces, batch, (grad,), (grad_all,), in_send, in_recv)
    begin_out, done_out = outward(axis, pieces, stage, landed, out_send, out_recv)

    def loading(n):
        slot = lax.rem(n, slots)
        return pltpu.make_async_copy(kern.at[n], tiles.at[slot], load.at[slot])

    @pl.when(w == 0)
    def _():
        hail(axis, pieces)
        for n in range(slots):
            loading(n).start()
        open_batches(axis, pieces, batch, (grad,), (grad_all,), begin_in)

    @pl.when(w > 0)
    def _():
        begin_out(w - 1)

    @pl.when(jnp.logical_and(w > 0, w - 1 + slots < own))
    def _():
        loading(w - 1 + slots).start()

    @pl.when(jnp.logical_and(w < own, lax.rem(w, own // batch) == 0))
    def _():
        arrive_in(w // (own // batch))

    @pl.when(w < own)
    def _():
        gather_pieces(draw, lambda k: grad_all[k, w], pieces, width)
        for j in range(blocks):
            split_scaled(vec, draw[j], prof[w, j, 1:2, :], j)
        loading(w).wait()
        slot = lax.rem(w, slots)
        sums = [None] * blocks
        for t, (i, j) in enumerate(tile_pairs(blocks)):
            tile = tiles[slot, t]
            sums[j] = add(sums[j], dot(vec[i], tile, NN))
            if j > i:
                turned[t] = tile.T
                sums[i] = add(sums[i], dot(vec[j], turned[t], NN))
        sums = joined(sums, lambda j: prof[w, j, 1:2, :], samples)
        keep_pieces(stage, w, sums, pieces, width)

    @pl.when(w == own)
    def _():
        sent_in()
        done_out()
        out[...] = landed[...]


def own_bins(label, at, start, samples):
    return jnp.broadcast_to(label[:, at], (samples, CHUNK)) - start


def field_group(samples, rows, data, own, pair):
    part = jnp.concatenate([rows[pair + i] for i in range(GROUP // 2)], axis=0)
    full = dot(part, data, NT)
    total = jnp.zeros((samples, CHUNK), jnp.float32)
    for b in range(GROUP):
        total = total + jnp.where(own == b, full[b * samples : (b + 1) * samples, :], 0.0)
    return total


def sums_group(value, data, own):
    full = jnp.concatenate([jnp.where(own == b, value, 0.0) for b in range(GROUP)], axis=0)
    return dot(full.astype(jnp.bfloat16), data, NN)


def chunk_at(c):
    return pl.ds(pl.multiple_of(c * CHUNK, CHUNK), CHUNK)


def fetch(basis, c, held, sem):
    copy = pltpu.make_async_copy(basis.at[chunk_at(c)], held, sem)
    copy.start()
    copy.wait()


def every(start, size, stride):
    return pl.ds(start, size, stride=stride)


def lane_pieces(width):
    piece = min(width, LANES)
    return [(k, slice(k * piece, (k + 1) * piece)) for k in range(width // piece)]


def filled(value):
    return jnp.concatenate([value] * (LANES // value.shape[1]), axis=1)


def spread_samples(wide_rows, source):
    waves, samples, width = source.shape
    for k, at in lane_pieces(width):
        flat = source[:, :, at].astype(jnp.float32).reshape(waves * samples, -1)
        wide_rows[k] = filled(flat)


def prepare_kernel(latent, length, amplitude_scale, draws, profile, wide_rows):
    samples, waves, width = latent.shape
    profile[:, 0, :] = length[...] * length[...]
    profile[:, 1, :] = amplitude_scale[...] * jnp.sqrt(math.sqrt(2.0) * length[...])
    for k, at in lane_pieces(width):
        for s in range(samples):
            wide_rows[k, every(s, waves, samples), :] = filled(latent[s, :, at].astype(jnp.float32))
        whole = wide_rows[k].reshape(waves, samples, LANES)
        draws[:, :, at] = whole[:, :, : min(width, LANES)].astype(draws.dtype)


def finish_kernel(pulled, latent, out, wide_rows):
    samples, waves, width = latent.shape
    spread_samples(wide_rows, pulled)
    for k, at in lane_pieces(width):
        for s in range(samples):
            value = wide_rows[k, every(s, waves, samples), :][:, : min(width, LANES)]
            out[s, :, at] = value + latent[s, :, at].astype(jnp.float32)


def rest_field_kernel(samples, chunks, pairs, trips, amp, label, basis, rows, extra, wide_rows, turned, held, sem):
    waves, _, width = amp.shape
    extra[...] = jnp.zeros_like(extra)
    spread_samples(wide_rows, amp)
    for k, at in lane_pieces(width):
        size = at.stop - at.start
        for s in range(samples):
            part = wide_rows[k, every(s, waves, samples), :].T[:size]
            turned[every(at.start * samples + s, size, samples), :] = part
    half = width // 2
    rows[:half] = turned[...].astype(rows.dtype).reshape(half, 2 * samples, waves)
    rows[half:] = jnp.zeros((GROUP // 2, 2 * samples, waves), rows.dtype)

    def over(c, _):
        start, count = pairs[c] * 2, trips[c]

        @pl.when(count > 1)
        def _():
            fetch(basis, c, held, sem)

            def more(k, total):
                first = start + k * GROUP
                own = own_bins(label, chunk_at(c), first, samples)
                return total + field_group(samples, rows, held[...], own, first // 2)

            extra[c] = lax.fori_loop(1, count, more, jnp.zeros((samples, CHUNK), jnp.float32))

        return 0

    lax.fori_loop(0, chunks, over, 0)


def rest_sums_kernel(
    samples, chunks, halves, per,
    pairs, trips, terms, weight, label, amp, yield_norm, basis, grad,
    sums, wide_rows, held, sem,
):
    waves, _, width = amp.shape
    sums[...] = jnp.zeros_like(sums)

    def put(start, term):
        sums[pl.ds(pl.multiple_of(start * samples, 2 * samples), GROUP * samples), :] += term

    def over(c, _):
        start, count = pairs[c] * 2, trips[c]
        put(start, terms[c])

        @pl.when(count > 1)
        def _():
            fetch(basis, c, held, sem)
            part, at = c // per, chunk_at(c % per)
            value = weight[part // halves, part % halves, :, at].astype(jnp.float32)

            def more(k, _):
                first = start + k * GROUP
                own = own_bins(label, chunk_at(c), first, samples)
                put(first, sums_group(value, held[...], own))
                return 0

            lax.fori_loop(1, count, more, 0)

        return 0

    lax.fori_loop(0, chunks, over, 0)
    spread_samples(wide_rows, amp)
    for k, at in lane_pieces(width):
        size = at.stop - at.start
        norm = filled(yield_norm[:, at]) * (2.0 / samples)
        for s in range(samples):
            mine = every(s, waves, samples)
            part = sums[every(at.start * samples + s, size, samples), :]
            part = jnp.concatenate([part] * (LANES // size), axis=0).T
            wide_rows[k, mine, :] = part + wide_rows[k, mine, :] * norm
        whole = wide_rows[k].reshape(waves, samples, LANES)
        grad[:, :, at] = whole[:, :, :size].astype(grad.dtype)


def events_kernel(
    axis, count, samples, halves, per,
    pairs, rows, label, extra, basis, terms, weight,
    held, partial, landed, send, recv, load,
):
    me = lax.axis_index(axis)
    parts = count * halves
    size = per * CHUNK

    def place(n):
        return lax.rem(me + 1 + lax.rem(n, count), count), n // count

    def loading(n):
        p, h = place(n)
        at = pl.ds(pl.multiple_of((p * halves + h) * size, size), size)
        return pltpu.make_async_copy(basis.at[at], held.at[at], load.at[n])

    def reducing(h, d):
        p = lax.rem(me + 1 + d, count)
        return remote(axis, p, partial.at[p, h], landed.at[d, h], send.at[0, h, d], recv.at[0, h, d])

    def sharing(h, d):
        p = lax.rem(me + 1 + d, count)
        return remote(axis, p, weight.at[me, h], weight.at[me, h], send.at[1, h, d], recv.at[1, h, d])

    ahead = min(2, parts)
    for n in range(ahead):
        loading(n).start()
    hail(axis, count)
    hear(count)

    def field(n, _):
        p, h = place(n)
        loading(n).wait()

        @pl.when(n + ahead < parts)
        def _():
            loading(n + ahead).start()

        for k in range(per):
            c = (p * halves + h) * per + k
            pair = pairs[c]
            own = own_bins(label, chunk_at(c), pair * 2, samples)
            total = extra[c] + field_group(samples, rows, held[chunk_at(c), :], own, pair)
            partial[p, h, :, k * CHUNK : (k + 1) * CHUNK] = total.astype(partial.dtype)

        @pl.when(lax.rem(n, count) < count - 1)
        def _():
            reducing(h, lax.rem(n, count)).start()

        return 0

    def sums(p, h):
        for k in range(per):
            c = (p * halves + h) * per + k
            own = own_bins(label, chunk_at(c), pairs[c] * 2, samples)
            value = weight[p, h, :, k * CHUNK : (k + 1) * CHUNK].astype(jnp.float32)
            terms[c] = sums_group(value, held[chunk_at(c), :], own)

    lax.fori_loop(0, parts, field, 0)

    def first(h, _):
        for d in range(count - 1):
            reducing(h, d).wait_recv()
        for k in range(per):
            at = slice(k * CHUNK, (k + 1) * CHUNK)
            total = partial[me, h, :, at].astype(jnp.float32)
            for d in range(count - 1):
                total = total + landed[d, h, :, at].astype(jnp.float32)
            weight[me, h, :, at] = (-2.0 * total / (1.0 + total * total) / samples).astype(weight.dtype)
        for d in range(count - 1):
            sharing(h, d).start()
        sums(me, h)
        return 0

    lax.fori_loop(0, halves, first, 0)

    def second(n, _):
        h, d = n // (count - 1), lax.rem(n, count - 1)
        sharing(h, d).wait_recv()
        sums(lax.rem(me + count - 1 - d, count), h)
        return 0

    lax.fori_loop(0, halves * (count - 1), second, 0)
    for h in range(halves):
        for d in range(count - 1):
            reducing(h, d).wait_send()
            sharing(h, d).wait_send()


def hail(axis, count):
    me, peers = around(axis, count)
    for peer in peers:
        pl.semaphore_signal(
            pltpu.get_barrier_semaphore(), inc=1, device_id={axis: peer}, device_id_type=MESH
        )


def hear(count):
    pl.semaphore_wait(pltpu.get_barrier_semaphore(), count - 1)


def params(**more):
    return pltpu.CompilerParams(
        dimension_semantics=("arbitrary",), vmem_limit_bytes=60 << 20, **more
    )


def shards(count, splits, latent, basis, event_bin, length, amplitude_scale, yield_norm, bin_coords):
    samples, waves, width = latent.shape
    total = bin_coords.shape[1]
    own = waves // count
    blocks = total // TILE
    tiles = blocks * (blocks + 1) // 2
    f32, bf16 = jnp.float32, jnp.bfloat16

    sheets = pltpu.VMEM((max(width // LANES, 1), waves * samples, LANES), f32)
    turned_shape = jax.ShapeDtypeStruct((waves, samples, width), bf16)

    def local(body, name, out_shape, in_specs, out_specs, scratch_shapes):
        return pl.pallas_call(
            body,
            out_shape=out_shape,
            in_specs=in_specs,
            out_specs=out_specs,
            scratch_shapes=scratch_shapes,
            compiler_params=pltpu.CompilerParams(vmem_limit_bytes=57 << 20),
            name=name,
        )

    vmem = pl.BlockSpec(memory_space=pltpu.VMEM)
    draws, profile = local(
        prepare_kernel,
        "prepare",
        (turned_shape, jax.ShapeDtypeStruct((waves, 2, width), f32)),
        [vmem] * 3,
        (vmem, vmem),
        [sheets],
    )(latent, length, amplitude_scale)
    profile = profile.reshape(count, own, 2, width)
    draws = draws.reshape(count, own, samples, width)

    batch = math.gcd(own, BATCHES)
    piece = jax.ShapeDtypeStruct((count, own, samples, width), bf16)
    kern_spec = pl.BlockSpec((1, tiles, TILE, TILE), lambda w: (jnp.minimum(w, own - 1), 0, 0, 0))
    stages = [
        pltpu.VMEM((own, count, samples, width), bf16),
        pltpu.VMEM((count, own, samples, width), bf16),
    ]

    def semaphores(arrays):
        return [
            pltpu.SemaphoreType.DMA((arrays,)),
            pltpu.SemaphoreType.DMA((arrays, batch)),
            pltpu.SemaphoreType.DMA,
            pltpu.SemaphoreType.DMA,
        ]

    events = basis.shape[0]
    chunks = events // CHUNK
    smem = pl.BlockSpec(memory_space=pltpu.SMEM)
    anywhere = pl.BlockSpec(memory_space=pltpu.HBM)
    marks = jax.ShapeDtypeStruct((chunks,), jnp.int32)
    kern, amp, kept, pairs, trips = pl.pallas_call(
        functools.partial(forward_kernel, "event", count, width, own, batch),
        out_shape=(
            jax.ShapeDtypeStruct((own, tiles, TILE, TILE), bf16),
            piece,
            jax.ShapeDtypeStruct((own, blocks, 2, TILE), f32),
            marks,
            marks,
        ),
        grid=(own + 1,),
        in_specs=[vmem, vmem, vmem, anywhere],
        out_specs=(kern_spec, vmem, vmem, smem, smem),
        scratch_shapes=[
            pltpu.VMEM((tiles, TILE, TILE), f32),
            pltpu.VMEM((total, LANES), f32),
            pltpu.VMEM((total, LANES), f32),
            pltpu.VMEM((blocks, 2, TILE), f32),
            pltpu.VMEM((blocks, 2, TILE), f32),
            pltpu.VMEM((blocks, samples, TILE), bf16),
            pltpu.VMEM((blocks, 2 * samples, TILE), bf16),
            pltpu.VMEM((count, own, 2, width), f32),
            pltpu.VMEM((count, own, samples, width), bf16),
        ]
        + stages
        + semaphores(2)
        + [pltpu.SMEM(event_bin.shape, jnp.int32), pltpu.SemaphoreType.DMA],
        compiler_params=params(collective_id=0, has_side_effects=True),
        name="kern_forward",
    )(bin_coords, profile, draws, event_bin)

    amp = amp.reshape(waves, samples, width)
    halves = math.gcd(chunks // splits, HALVES)
    per = chunks // splits // halves
    one = [pltpu.VMEM((CHUNK, waves), bf16), pltpu.SemaphoreType.DMA]
    amp_rows, extra = local(
        functools.partial(rest_field_kernel, samples, chunks),
        "rest_field",
        (
            jax.ShapeDtypeStruct(((width + GROUP) // 2, 2 * samples, waves), bf16),
            jax.ShapeDtypeStruct((chunks, samples, CHUNK), f32),
        ),
        [smem, smem, vmem, vmem, anywhere],
        (vmem, vmem),
        [sheets, pltpu.VMEM((width * samples, waves), f32)] + one,
    )(pairs, trips, amp, event_bin, basis)
    shared = (splits, halves, samples, per * CHUNK)
    terms, weight = pl.pallas_call(
        functools.partial(events_kernel, "wave", splits, samples, halves, per),
        out_shape=(
            jax.ShapeDtypeStruct((chunks, GROUP * samples, waves), f32),
            jax.ShapeDtypeStruct(shared, bf16),
        ),
        in_specs=[smem, vmem, vmem, vmem, anywhere],
        out_specs=(vmem, vmem),
        scratch_shapes=[
            pltpu.VMEM((events, waves), bf16),
            pltpu.VMEM(shared, bf16),
            pltpu.VMEM((splits - 1,) + shared[1:], bf16),
            pltpu.SemaphoreType.DMA((2, halves, splits - 1)),
            pltpu.SemaphoreType.DMA((2, halves, splits - 1)),
            pltpu.SemaphoreType.DMA((splits * halves,)),
        ],
        compiler_params=pltpu.CompilerParams(
            collective_id=2, has_side_effects=True, vmem_limit_bytes=57 << 20
        ),
        name="events",
    )(pairs, amp_rows, event_bin, extra, basis)
    grad = local(
        functools.partial(rest_sums_kernel, samples, chunks, halves, per),
        "rest_sums",
        turned_shape,
        [smem, smem] + [vmem] * 5 + [anywhere],
        vmem,
        [pltpu.VMEM(((width + GROUP) * samples, waves), f32), sheets] + one,
    )(pairs, trips, terms, weight, event_bin, amp, yield_norm, basis)
    slots = min(own, AHEAD)
    pulled = pl.pallas_call(
        functools.partial(backward_kernel, "event", count, width, own, batch, slots),
        out_shape=piece,
        grid=(own + 1,),
        in_specs=[anywhere, vmem, vmem],
        out_specs=vmem,
        scratch_shapes=[
            pltpu.VMEM((slots, tiles, TILE, TILE), bf16),
            pltpu.VMEM((tiles, TILE, TILE), bf16),
            pltpu.VMEM((blocks, samples, TILE), bf16),
            pltpu.VMEM((blocks, 2 * samples, TILE), bf16),
            pltpu.VMEM((count, own, samples, width), bf16),
        ]
        + stages
        + [pltpu.SemaphoreType.DMA((slots,))]
        + semaphores(1),
        compiler_params=params(collective_id=1, has_side_effects=True),
        name="kern_backward",
    )(kern, grad.reshape(count, own, samples, width), kept)
    return local(
        finish_kernel,
        "finish",
        jax.ShapeDtypeStruct(latent.shape, f32),
        [vmem, vmem],
        vmem,
        [sheets],
    )(pulled.reshape(waves, samples, width), latent)


def solution(mesh):
    placed = (
        P(None, "wave", "event"),
        P("event", "wave"),
        P("event", None),
        P("wave", "event"),
        P("wave", "event"),
        P("wave", "event"),
        P(),
    )
    return jax.shard_map(
        functools.partial(shards, mesh.shape["event"], mesh.shape["wave"]),
        mesh=mesh,
        in_specs=placed,
        out_specs=P(None, "wave", "event"),
        check_vma=False,
    )
```

```python
import functools
import math

import jax
import jax.numpy as jnp
from jax import lax
from jax.experimental import pallas as pl
from jax.experimental.pallas import tpu as pltpu
from jax.sharding import PartitionSpec as P

TILE = 256
LANES = 128
CHUNK = 1024
GROUP = 24
BATCHES = 16
HALVES = 2
AHEAD = 8
MESH = pl.DeviceIdType.MESH
NN = (((1,), (0,)), ((), ()))
NT = (((1,), (1,)), ((), ()))


def dot(a, b, dims):
    return lax.dot_general(a, b, dims, preferred_element_type=jnp.float32)


def spread_rows(dst, read, total):
    for k in range(total // LANES):
        row = read(k * LANES)
        dst[pl.ds(k * LANES, LANES), :] = jnp.broadcast_to(row, (LANES, LANES)).T


def gather_pieces(dst, src, pieces, width):
    for k in range(pieces):
        block, lane = (k * width) // TILE, (k * width) % TILE
        dst[block, :, lane : lane + width] = src(k)


def wide(column):
    return jnp.concatenate([column] * (TILE // LANES), axis=1)


def tile_pairs(blocks):
    return [(i, j) for i in range(blocks) for j in range(i, blocks)]


def add(held, term):
    return term if held is None else held + term


def multiply(sums, vec, tile, i, j):
    sums[j] = add(sums[j], dot(vec[i], tile, NN))
    if j > i:
        sums[i] = add(sums[i], dot(vec[j], tile, NT))


def keep_pieces(dst, slot, sums, pieces, width):
    for k in range(pieces):
        block, lane = (k * width) // TILE, (k * width) % TILE
        dst[slot, k] = sums[block][:, lane : lane + width].astype(dst.dtype)


def around(axis, count):
    me = lax.axis_index(axis)
    return me, [lax.rem(me + d, count) for d in range(1, count)]


def remote(axis, peer, src, dst, send, recv):
    return pltpu.make_async_remote_copy(
        src_ref=src,
        dst_ref=dst,
        send_sem=send,
        recv_sem=recv,
        device_id={axis: peer},
        device_id_type=MESH,
    )


def bytes_of(ref, sem):
    return pltpu.make_async_copy(ref, ref, sem)


def inward(axis, count, batch, sources, targets, send, recv):
    me, peers = around(axis, count)
    size = sources[0].shape[1] // batch

    def begin(q):
        at = pl.ds(q * size, size)
        for peer in peers:
            for a, (src, dst) in enumerate(zip(sources, targets)):
                remote(axis, peer, src.at[peer, at], dst.at[me, at], send.at[a], recv.at[a, q]).start()

    def arrive(q):
        for a, dst in enumerate(targets):
            bytes_of(dst.at[pl.ds(0, count - 1), pl.ds(q * size, size)], recv.at[a, q]).wait()

    def sent():
        for a, src in enumerate(sources):
            bytes_of(src.at[pl.ds(0, count - 1)], send.at[a]).wait()

    return begin, arrive, sent


def outward(axis, count, stage, landed, send, recv):
    me, peers = around(axis, count)

    def begin(w):
        for peer in peers:
            remote(axis, peer, stage.at[w, peer], landed.at[me, w], send, recv).start()
        landed[me, w] = stage[w, me]

    def done():
        whole = landed.at[pl.ds(0, count - 1)]
        bytes_of(whole, send).wait()
        bytes_of(whole, recv).wait()

    return begin, done


def open_batches(axis, count, batch, sources, targets, begin):
    me = lax.axis_index(axis)
    hear(count)
    for q in range(batch):
        begin(q)
    for src, dst in zip(sources, targets):
        dst[me] = src[me]


def split_scaled(vec, value, scale, at):
    whole = value.astype(jnp.float32) * scale
    high = whole.astype(vec.dtype)
    low = (whole - high.astype(jnp.float32)).astype(vec.dtype)
    vec[at] = jnp.concatenate([high, low], axis=0)


def joined(sums, scale, samples):
    return [
        (part[:samples] + part[samples:]) * scale(block) for block, part in enumerate(sums)
    ]


def every(start, size, stride):
    return pl.ds(start, size, stride=stride)


def lane_pieces(width):
    piece = min(width, LANES)
    return [(k, slice(k * piece, (k + 1) * piece)) for k in range(width // piece)]


def filled(value):
    return jnp.concatenate([value] * (LANES // value.shape[1]), axis=1)


def spread_samples(wide_rows, source):
    waves, samples, width = source.shape
    for k, at in lane_pieces(width):
        flat = source[:, :, at].astype(jnp.float32).reshape(waves * samples, -1)
        wide_rows[k] = filled(flat)


def prepare(latent, length, amplitude_scale, draws, profile, wide_rows):
    samples, waves, width = latent.shape
    pieces, own = draws.shape[:2]
    square = length[...] * length[...]
    scale = amplitude_scale[...] * jnp.sqrt(math.sqrt(2.0) * length[...])
    for p in range(pieces):
        mine = slice(p * own, (p + 1) * own)
        profile[p, :, 0, :] = square[mine]
        profile[p, :, 1, :] = scale[mine]
    for k, at in lane_pieces(width):
        for s in range(samples):
            wide_rows[k, every(s, waves, samples), :] = filled(latent[s, :, at].astype(jnp.float32))
        whole = wide_rows[k].reshape(waves, samples, LANES)[:, :, : min(width, LANES)]
        for p in range(pieces):
            draws[p, :, :, at] = whole[p * own : (p + 1) * own].astype(draws.dtype)


def turn_rows(amp, rows, wide_rows, turned):
    waves, samples, width = amp.shape
    for k, at in lane_pieces(width):
        flat = amp[:, :, at].astype(jnp.float32).reshape(waves * samples, -1)
        wide_rows[k] = filled(flat)
        size = at.stop - at.start
        for s in range(samples):
            part = wide_rows[k, every(s, waves, samples), :].T[:size]
            turned[every(at.start * samples + s, size, samples), :] = part
    half = width // 2
    rows[:half] = turned[...].astype(rows.dtype).reshape(half, 2 * samples, waves)
    rows[half:] = jnp.zeros((GROUP // 2, 2 * samples, waves), rows.dtype)


def forward_kernel(
    axis, pieces, width, own, batch,
    coords, latents, length, amplitude_scale, label, kern, amp, rows, kept, pairs, trips,
    profile, latent, wide_rows, turned, dist, col_x, col_y, prof, later, draw, vec, prof_all, draws_all, stage, landed,
    in_send, in_recv, out_send, out_recv, bins, mark,
):
    total = pieces * width
    blocks = total // TILE
    samples = latent.shape[2]
    step = 64
    per = own // batch
    w = pl.program_id(0)
    sources, targets = (profile, latent), (prof_all, draws_all)
    begin_in, arrive_in, sent_in = inward(axis, pieces, batch, sources, targets, in_send, in_recv)
    begin_out, done_out = outward(axis, pieces, stage, landed, out_send, out_recv)

    marking = pltpu.make_async_copy(label, bins, mark)

    def read_marks():
        marking.wait()

        def over(c, _):
            pair = lax.shift_right_logical(bins[0, c * CHUNK], 1)
            pairs[c] = pair
            trips[c] = (bins[0, c * CHUNK + CHUNK - 1] - pair * 2) // GROUP + 1
            return 0

        lax.fori_loop(0, pairs.shape[0], over, 0)

    def entries(i, j, t, r, rows, c, cols):
        own_x = col_x[pl.ds(i * TILE + r, rows), :]
        square = jnp.concatenate([own_x] * (cols // LANES), axis=1) + prof[j, 0:1, c : c + cols]
        root = lax.rsqrt(square)
        return root * jnp.exp2(dist[t, r : r + rows, c : c + cols] * (root * root))

    @pl.when(w == 0)
    def _():
        hail(axis, pieces)
        marking.start()
        prepare(latents, length, amplitude_scale, latent, profile, wide_rows)
        spread_rows(col_x, lambda k: coords[0:1, k : k + LANES], total)
        spread_rows(col_y, lambda k: coords[1:2, k : k + LANES], total)
        open_batches(axis, pieces, batch, sources, targets, begin_in)

        def over_i(i, t0):
            def over_j(j, t):
                col = pl.ds(pl.multiple_of(j * TILE, TILE), TILE)
                x_c, y_c = coords[0:1, col], coords[1:2, col]
                for r in range(0, TILE, step):
                    row = pl.ds(pl.multiple_of(i * TILE + r, step), step)
                    dx = wide(col_x[row, :]) - x_c
                    dy = wide(col_y[row, :]) - y_c
                    dist[t, r : r + step, :] = (dx * dx + dy * dy) * (-math.log2(math.e))
                return t + 1

            return lax.fori_loop(i, blocks, over_j, t0)

        lax.fori_loop(0, blocks, over_i, 0)
        arrive_in(0)
        gather_pieces(later, lambda k: prof_all[k, 0], pieces, width)
        spread_rows(col_x, lambda k: later[k // TILE, 0:1, k % TILE : k % TILE + LANES], total)

    @pl.when(w > 0)
    def _():
        begin_out(w - 1)

    @pl.when(jnp.logical_and(w + 1 < own, lax.rem(w + 1, per) == 0))
    def _():
        arrive_in((w + 1) // per)

    @pl.when(w < own)
    def _():
        after = jnp.minimum(w + 1, own - 1)
        gather_pieces(prof, lambda k: prof_all[k, w], pieces, width)
        gather_pieces(later, lambda k: prof_all[k, after], pieces, width)
        gather_pieces(draw, lambda k: draws_all[k, w], pieces, width)
        kept[w] = prof[...]
        for j in range(blocks):
            split_scaled(vec, draw[j], prof[j, 1:2, :], j)
        sums = [None] * blocks
        for t, (i, j) in sorted(enumerate(tile_pairs(blocks)), key=lambda p: (-p[1][0], p[1][1])):
            if i == j:
                upper = entries(i, j, t, 0, LANES, 0, TILE)
                lower = entries(i, j, t, LANES, LANES, LANES, LANES)
                lower = jnp.concatenate([upper[:, LANES:].T, lower], axis=1)
                strips = [upper.astype(jnp.bfloat16), lower.astype(jnp.bfloat16)]
            else:
                strips = [
                    entries(i, j, t, r, step, 0, TILE).astype(jnp.bfloat16)
                    for r in range(0, TILE, step)
                ]
            tile = jnp.concatenate(strips, axis=0)
            kern[0, t] = tile
            multiply(sums, vec, tile, i, j)
            if j == blocks - 1:
                for k in range(0, TILE, LANES):
                    row = later[i, 0:1, k : k + LANES]
                    at = pl.ds(i * TILE + k, LANES)
                    col_x[at, :] = jnp.broadcast_to(row, (LANES, LANES)).T
        sums = joined(sums, lambda j: prof[j, 1:2, :], samples)
        keep_pieces(stage, w, sums, pieces, width)

    @pl.when(w == own)
    def _():
        read_marks()
        sent_in()
        done_out()
        whole = landed[...].reshape(amp.shape)
        amp[...] = whole
        turn_rows(whole, rows, wide_rows, turned)


def backward_kernel(
    axis, pieces, width, own, batch, slots,
    kern, grad, prof, out,
    tiles, turned, draw, vec, grad_all, stage, landed, load, in_send, in_recv, out_send, out_recv,
):
    total = pieces * width
    blocks = total // TILE
    samples = grad.shape[2]
    w = pl.program_id(0)
    begin_in, arrive_in, sent_in = inward(axis, pieces, batch, (grad,), (grad_all,), in_send, in_recv)
    begin_out, done_out = outward(axis, pieces, stage, landed, out_send, out_recv)

    def loading(n):
        slot = lax.rem(n, slots)
        return pltpu.make_async_copy(kern.at[n], tiles.at[slot], load.at[slot])

    @pl.when(w == 0)
    def _():
        hail(axis, pieces)
        for n in range(slots):
            loading(n).start()
        open_batches(axis, pieces, batch, (grad,), (grad_all,), begin_in)

    @pl.when(w > 0)
    def _():
        begin_out(w - 1)

    @pl.when(jnp.logical_and(w > 0, w - 1 + slots < own))
    def _():
        loading(w - 1 + slots).start()

    @pl.when(jnp.logical_and(w < own, lax.rem(w, own // batch) == 0))
    def _():
        arrive_in(w // (own // batch))

    @pl.when(w < own)
    def _():
        gather_pieces(draw, lambda k: grad_all[k, w], pieces, width)
        for j in range(blocks):
            split_scaled(vec, draw[j], prof[w, j, 1:2, :], j)
        loading(w).wait()
        slot = lax.rem(w, slots)
        sums = [None] * blocks
        for t, (i, j) in enumerate(tile_pairs(blocks)):
            tile = tiles[slot, t]
            sums[j] = add(sums[j], dot(vec[i], tile, NN))
            if j > i:
                turned[t] = tile.T
                sums[i] = add(sums[i], dot(vec[j], turned[t], NN))
        sums = joined(sums, lambda j: prof[w, j, 1:2, :], samples)
        keep_pieces(stage, w, sums, pieces, width)

    @pl.when(w == own)
    def _():
        sent_in()
        done_out()
        out[...] = landed[...]


def own_bins(label, at, start, samples):
    return jnp.broadcast_to(label[:, at], (samples, CHUNK)) - start


def field_group(samples, rows, data, own, pair):
    part = jnp.concatenate([rows[pair + i] for i in range(GROUP // 2)], axis=0)
    full = dot(part, data, NT)
    total = jnp.zeros((samples, CHUNK), jnp.float32)
    for b in range(GROUP):
        total = total + jnp.where(own == b, full[b * samples : (b + 1) * samples, :], 0.0)
    return total


def sums_group(value, data, own):
    full = jnp.concatenate([jnp.where(own == b, value, 0.0) for b in range(GROUP)], axis=0)
    return dot(full.astype(jnp.bfloat16), data, NN)


def chunk_at(c):
    return pl.ds(pl.multiple_of(c * CHUNK, CHUNK), CHUNK)


def fetch(basis, c, held, sem):
    copy = pltpu.make_async_copy(basis.at[chunk_at(c)], held, sem)
    copy.start()
    copy.wait()


def finish_kernel(pulled, latent, out, wide_rows):
    samples, waves, width = latent.shape
    spread_samples(wide_rows, pulled)
    for k, at in lane_pieces(width):
        for s in range(samples):
            value = wide_rows[k, every(s, waves, samples), :][:, : min(width, LANES)]
            out[s, :, at] = value + latent[s, :, at].astype(jnp.float32)


def rest_field_kernel(samples, chunks, pairs, trips, rows, label, basis, extra, held, sem):
    extra[...] = jnp.zeros_like(extra)

    def over(c, _):
        start, count = pairs[c] * 2, trips[c]

        @pl.when(count > 1)
        def _():
            fetch(basis, c, held, sem)

            def more(k, total):
                first = start + k * GROUP
                own = own_bins(label, chunk_at(c), first, samples)
                return total + field_group(samples, rows, held[...], own, first // 2)

            extra[c] = lax.fori_loop(1, count, more, jnp.zeros((samples, CHUNK), jnp.float32))

        return 0

    lax.fori_loop(0, chunks, over, 0)


def rest_sums_kernel(
    samples, chunks, halves, per,
    pairs, trips, terms, weight, label, amp, yield_norm, basis, grad,
    sums, wide_rows, held, sem,
):
    waves, _, width = amp.shape
    sums[...] = jnp.zeros_like(sums)

    def put(start, term):
        sums[pl.ds(pl.multiple_of(start * samples, 2 * samples), GROUP * samples), :] += term

    def over(c, _):
        start, count = pairs[c] * 2, trips[c]
        put(start, terms[c])

        @pl.when(count > 1)
        def _():
            fetch(basis, c, held, sem)
            part, at = c // per, chunk_at(c % per)
            value = weight[part // halves, part % halves, :, at].astype(jnp.float32)

            def more(k, _):
                first = start + k * GROUP
                own = own_bins(label, chunk_at(c), first, samples)
                put(first, sums_group(value, held[...], own))
                return 0

            lax.fori_loop(1, count, more, 0)

        return 0

    lax.fori_loop(0, chunks, over, 0)
    spread_samples(wide_rows, amp)
    for k, at in lane_pieces(width):
        size = at.stop - at.start
        norm = filled(yield_norm[:, at]) * (2.0 / samples)
        for s in range(samples):
            mine = every(s, waves, samples)
            part = sums[every(at.start * samples + s, size, samples), :]
            part = jnp.concatenate([part] * (LANES // size), axis=0).T
            wide_rows[k, mine, :] = part + wide_rows[k, mine, :] * norm
        whole = wide_rows[k].reshape(waves, samples, LANES)
        grad[:, :, at] = whole[:, :, :size].astype(grad.dtype)


def events_kernel(
    axis, count, samples, halves, per,
    pairs, rows, label, extra, basis, terms, weight,
    held, partial, landed, send, recv, load,
):
    me = lax.axis_index(axis)
    parts = count * halves
    size = per * CHUNK

    def place(n):
        return lax.rem(me + 1 + lax.rem(n, count), count), n // count

    def loading(n):
        p, h = place(n)
        at = pl.ds(pl.multiple_of((p * halves + h) * size, size), size)
        return pltpu.make_async_copy(basis.at[at], held.at[at], load.at[n])

    def reducing(h, d):
        p = lax.rem(me + 1 + d, count)
        return remote(axis, p, partial.at[p, h], landed.at[d, h], send.at[0, h, d], recv.at[0, h, d])

    def sharing(h, d):
        p = lax.rem(me + 1 + d, count)
        return remote(axis, p, weight.at[me, h], weight.at[me, h], send.at[1, h, d], recv.at[1, h, d])

    ahead = min(2, parts)
    for n in range(ahead):
        loading(n).start()
    hail(axis, count)
    hear(count)

    def field(n, _):
        p, h = place(n)
        loading(n).wait()

        @pl.when(n + ahead < parts)
        def _():
            loading(n + ahead).start()

        for k in range(per):
            c = (p * halves + h) * per + k
            pair = pairs[c]
            own = own_bins(label, chunk_at(c), pair * 2, samples)
            total = extra[c] + field_group(samples, rows, held[chunk_at(c), :], own, pair)
            partial[p, h, :, k * CHUNK : (k + 1) * CHUNK] = total.astype(partial.dtype)

        @pl.when(lax.rem(n, count) < count - 1)
        def _():
            reducing(h, lax.rem(n, count)).start()

        return 0

    def sums(p, h):
        for k in range(per):
            c = (p * halves + h) * per + k
            own = own_bins(label, chunk_at(c), pairs[c] * 2, samples)
            value = weight[p, h, :, k * CHUNK : (k + 1) * CHUNK].astype(jnp.float32)
            terms[c] = sums_group(value, held[chunk_at(c), :], own)

    lax.fori_loop(0, parts, field, 0)

    def first(h, _):
        for d in range(count - 1):
            reducing(h, d).wait_recv()
        for k in range(per):
            at = slice(k * CHUNK, (k + 1) * CHUNK)
            total = partial[me, h, :, at].astype(jnp.float32)
            for d in range(count - 1):
                total = total + landed[d, h, :, at].astype(jnp.float32)
            weight[me, h, :, at] = (-2.0 * total / (1.0 + total * total) / samples).astype(weight.dtype)
        for d in range(count - 1):
            sharing(h, d).start()
        sums(me, h)
        return 0

    lax.fori_loop(0, halves, first, 0)

    def second(n, _):
        h, d = n // (count - 1), lax.rem(n, count - 1)
        sharing(h, d).wait_recv()
        sums(lax.rem(me + count - 1 - d, count), h)
        return 0

    lax.fori_loop(0, halves * (count - 1), second, 0)
    for h in range(halves):
        for d in range(count - 1):
            reducing(h, d).wait_send()
            sharing(h, d).wait_send()


def hail(axis, count):
    me, peers = around(axis, count)
    for peer in peers:
        pl.semaphore_signal(
            pltpu.get_barrier_semaphore(), inc=1, device_id={axis: peer}, device_id_type=MESH
        )


def hear(count):
    pl.semaphore_wait(pltpu.get_barrier_semaphore(), count - 1)


def params(**more):
    return pltpu.CompilerParams(
        dimension_semantics=("arbitrary",), vmem_limit_bytes=60 << 20, **more
    )


def shards(count, splits, latent, basis, event_bin, length, amplitude_scale, yield_norm, bin_coords):
    samples, waves, width = latent.shape
    total = bin_coords.shape[1]
    own = waves // count
    blocks = total // TILE
    tiles = blocks * (blocks + 1) // 2
    f32, bf16 = jnp.float32, jnp.bfloat16

    sheets = pltpu.VMEM((max(width // LANES, 1), waves * samples, LANES), f32)
    turned_shape = jax.ShapeDtypeStruct((waves, samples, width), bf16)

    def local(body, name, out_shape, in_specs, out_specs, scratch_shapes):
        return pl.pallas_call(
            body,
            out_shape=out_shape,
            in_specs=in_specs,
            out_specs=out_specs,
            scratch_shapes=scratch_shapes,
            compiler_params=pltpu.CompilerParams(vmem_limit_bytes=57 << 20),
            name=name,
        )

    vmem = pl.BlockSpec(memory_space=pltpu.VMEM)
    batch = math.gcd(own, BATCHES)
    piece = jax.ShapeDtypeStruct((count, own, samples, width), bf16)
    kern_spec = pl.BlockSpec((1, tiles, TILE, TILE), lambda w: (jnp.minimum(w, own - 1), 0, 0, 0))
    stages = [
        pltpu.VMEM((own, count, samples, width), bf16),
        pltpu.VMEM((count, own, samples, width), bf16),
    ]

    def semaphores(arrays):
        return [
            pltpu.SemaphoreType.DMA((arrays,)),
            pltpu.SemaphoreType.DMA((arrays, batch)),
            pltpu.SemaphoreType.DMA,
            pltpu.SemaphoreType.DMA,
        ]

    events = basis.shape[0]
    chunks = events // CHUNK
    smem = pl.BlockSpec(memory_space=pltpu.SMEM)
    anywhere = pl.BlockSpec(memory_space=pltpu.HBM)
    marks = jax.ShapeDtypeStruct((chunks,), jnp.int32)
    kern, amp, amp_rows, kept, pairs, trips = pl.pallas_call(
        functools.partial(forward_kernel, "event", count, width, own, batch),
        out_shape=(
            jax.ShapeDtypeStruct((own, tiles, TILE, TILE), bf16),
            turned_shape,
            jax.ShapeDtypeStruct(((width + GROUP) // 2, 2 * samples, waves), bf16),
            jax.ShapeDtypeStruct((own, blocks, 2, TILE), f32),
            marks,
            marks,
        ),
        grid=(own + 1,),
        in_specs=[vmem, vmem, vmem, vmem, anywhere],
        out_specs=(kern_spec, vmem, vmem, vmem, smem, smem),
        scratch_shapes=[
            pltpu.VMEM((count, own, 2, width), f32),
            pltpu.VMEM((count, own, samples, width), bf16),
            sheets,
            pltpu.VMEM((width * samples, waves), f32),
            pltpu.VMEM((tiles, TILE, TILE), f32),
            pltpu.VMEM((total, LANES), f32),
            pltpu.VMEM((total, LANES), f32),
            pltpu.VMEM((blocks, 2, TILE), f32),
            pltpu.VMEM((blocks, 2, TILE), f32),
            pltpu.VMEM((blocks, samples, TILE), bf16),
            pltpu.VMEM((blocks, 2 * samples, TILE), bf16),
            pltpu.VMEM((count, own, 2, width), f32),
            pltpu.VMEM((count, own, samples, width), bf16),
        ]
        + stages
        + semaphores(2)
        + [pltpu.SMEM(event_bin.shape, jnp.int32), pltpu.SemaphoreType.DMA],
        compiler_params=params(collective_id=0, has_side_effects=True),
        name="kern_forward",
    )(bin_coords, latent, length, amplitude_scale, event_bin)

    halves = math.gcd(chunks // splits, HALVES)
    per = chunks // splits // halves
    one = [pltpu.VMEM((CHUNK, waves), bf16), pltpu.SemaphoreType.DMA]
    extra = local(
        functools.partial(rest_field_kernel, samples, chunks),
        "rest_field",
        jax.ShapeDtypeStruct((chunks, samples, CHUNK), f32),
        [smem, smem, vmem, vmem, anywhere],
        vmem,
        one,
    )(pairs, trips, amp_rows, event_bin, basis)
    shared = (splits, halves, samples, per * CHUNK)
    terms, weight = pl.pallas_call(
        functools.partial(events_kernel, "wave", splits, samples, halves, per),
        out_shape=(
            jax.ShapeDtypeStruct((chunks, GROUP * samples, waves), f32),
            jax.ShapeDtypeStruct(shared, bf16),
        ),
        in_specs=[smem, vmem, vmem, vmem, anywhere],
        out_specs=(vmem, vmem),
        scratch_shapes=[
            pltpu.VMEM((events, waves), bf16),
            pltpu.VMEM(shared, bf16),
            pltpu.VMEM((splits - 1,) + shared[1:], bf16),
            pltpu.SemaphoreType.DMA((2, halves, splits - 1)),
            pltpu.SemaphoreType.DMA((2, halves, splits - 1)),
            pltpu.SemaphoreType.DMA((splits * halves,)),
        ],
        compiler_params=pltpu.CompilerParams(
            collective_id=2, has_side_effects=True, vmem_limit_bytes=57 << 20
        ),
        name="events",
    )(pairs, amp_rows, event_bin, extra, basis)
    grad = local(
        functools.partial(rest_sums_kernel, samples, chunks, halves, per),
        "rest_sums",
        turned_shape,
        [smem, smem] + [vmem] * 5 + [anywhere],
        vmem,
        [pltpu.VMEM(((width + GROUP) * samples, waves), f32), sheets] + one,
    )(pairs, trips, terms, weight, event_bin, amp, yield_norm, basis)
    slots = min(own, AHEAD)
    pulled = pl.pallas_call(
        functools.partial(backward_kernel, "event", count, width, own, batch, slots),
        out_shape=piece,
        grid=(own + 1,),
        in_specs=[anywhere, vmem, vmem],
        out_specs=vmem,
        scratch_shapes=[
            pltpu.VMEM((slots, tiles, TILE, TILE), bf16),
            pltpu.VMEM((tiles, TILE, TILE), bf16),
            pltpu.VMEM((blocks, samples, TILE), bf16),
            pltpu.VMEM((blocks, 2 * samples, TILE), bf16),
            pltpu.VMEM((count, own, samples, width), bf16),
        ]
        + stages
        + [pltpu.SemaphoreType.DMA((slots,))]
        + semaphores(1),
        compiler_params=params(collective_id=1, has_side_effects=True),
        name="kern_backward",
    )(kern, grad.reshape(count, own, samples, width), kept)
    return local(
        finish_kernel,
        "finish",
        jax.ShapeDtypeStruct(latent.shape, f32),
        [vmem, vmem],
        vmem,
        [sheets],
    )(pulled.reshape(waves, samples, width), latent)


def solution(mesh):
    placed = (
        P(None, "wave", "event"),
        P("event", "wave"),
        P("event", None),
        P("wave", "event"),
        P("wave", "event"),
        P("wave", "event"),
        P(),
    )
    return jax.shard_map(
        functools.partial(shards, mesh.shape["event"], mesh.shape["wave"]),
        mesh=mesh,
        in_specs=placed,
        out_specs=P(None, "wave", "event"),
        check_vma=False,
    )
```

```python
import functools
import math

import jax
import jax.numpy as jnp
from jax import lax
from jax.experimental import pallas as pl
from jax.experimental.pallas import tpu as pltpu
from jax.sharding import PartitionSpec as P

TILE = 256
LANES = 128
CHUNK = 1024
GROUP = 24
BATCHES = 16
HALVES = 2
AHEAD = 8
MESH = pl.DeviceIdType.MESH
NN = (((1,), (0,)), ((), ()))
NT = (((1,), (1,)), ((), ()))


def dot(a, b, dims):
    return lax.dot_general(a, b, dims, preferred_element_type=jnp.float32)


def spread_rows(dst, read, total):
    for k in range(total // LANES):
        row = read(k * LANES)
        dst[pl.ds(k * LANES, LANES), :] = jnp.broadcast_to(row, (LANES, LANES)).T


def gather_pieces(dst, src, pieces, width):
    for k in range(pieces):
        block, lane = (k * width) // TILE, (k * width) % TILE
        dst[block, :, lane : lane + width] = src(k)


def wide(column):
    return jnp.concatenate([column] * (TILE // LANES), axis=1)


def tile_pairs(blocks):
    return [(i, j) for i in range(blocks) for j in range(i, blocks)]


def add(held, term):
    return term if held is None else held + term


def multiply(sums, vec, tile, i, j):
    sums[j] = add(sums[j], dot(vec[i], tile, NN))
    if j > i:
        sums[i] = add(sums[i], dot(vec[j], tile, NT))


def keep_pieces(dst, slot, sums, pieces, width):
    for k in range(pieces):
        block, lane = (k * width) // TILE, (k * width) % TILE
        dst[slot, k] = sums[block][:, lane : lane + width].astype(dst.dtype)


def around(axis, count):
    me = lax.axis_index(axis)
    return me, [lax.rem(me + d, count) for d in range(1, count)]


def remote(axis, peer, src, dst, send, recv):
    return pltpu.make_async_remote_copy(
        src_ref=src,
        dst_ref=dst,
        send_sem=send,
        recv_sem=recv,
        device_id={axis: peer},
        device_id_type=MESH,
    )


def bytes_of(ref, sem):
    return pltpu.make_async_copy(ref, ref, sem)


def inward(axis, count, batch, sources, targets, send, recv):
    me, peers = around(axis, count)
    size = sources[0].shape[1] // batch

    def begin(q):
        at = pl.ds(q * size, size)
        for peer in peers:
            for a, (src, dst) in enumerate(zip(sources, targets)):
                remote(axis, peer, src.at[peer, at], dst.at[me, at], send.at[a], recv.at[a, q]).start()

    def arrive(q):
        for a, dst in enumerate(targets):
            bytes_of(dst.at[pl.ds(0, count - 1), pl.ds(q * size, size)], recv.at[a, q]).wait()

    def sent():
        for a, src in enumerate(sources):
            bytes_of(src.at[pl.ds(0, count - 1)], send.at[a]).wait()

    return begin, arrive, sent


def outward(axis, count, stage, landed, send, recv):
    me, peers = around(axis, count)

    def begin(w):
        for peer in peers:
            remote(axis, peer, stage.at[w, peer], landed.at[me, w], send, recv).start()
        landed[me, w] = stage[w, me]

    def done():
        whole = landed.at[pl.ds(0, count - 1)]
        bytes_of(whole, send).wait()
        bytes_of(whole, recv).wait()

    return begin, done


def open_batches(axis, count, batch, sources, targets, begin):
    me = lax.axis_index(axis)
    hear(count)
    for q in range(batch):
        begin(q)
    for src, dst in zip(sources, targets):
        dst[me] = src[me]


def split_scaled(vec, value, scale, at):
    whole = value.astype(jnp.float32) * scale
    high = whole.astype(vec.dtype)
    low = (whole - high.astype(jnp.float32)).astype(vec.dtype)
    vec[at] = jnp.concatenate([high, low], axis=0)


def joined(sums, scale, samples):
    return [
        (part[:samples] + part[samples:]) * scale(block) for block, part in enumerate(sums)
    ]


def every(start, size, stride):
    return pl.ds(start, size, stride=stride)


def lane_pieces(width):
    piece = min(width, LANES)
    return [(k, slice(k * piece, (k + 1) * piece)) for k in range(width // piece)]


def filled(value):
    return jnp.concatenate([value] * (LANES // value.shape[1]), axis=1)


def spread_samples(wide_rows, source):
    waves, samples, width = source.shape
    for k, at in lane_pieces(width):
        flat = source[:, :, at].astype(jnp.float32).reshape(waves * samples, -1)
        wide_rows[k] = filled(flat)


def prepare(latent, length, amplitude_scale, draws, profile, wide_rows):
    samples, waves, width = latent.shape
    pieces, own = draws.shape[:2]
    square = length[...] * length[...]
    scale = amplitude_scale[...] * jnp.sqrt(math.sqrt(2.0) * length[...])
    for p in range(pieces):
        mine = slice(p * own, (p + 1) * own)
        profile[p, :, 0, :] = square[mine]
        profile[p, :, 1, :] = scale[mine]
    for k, at in lane_pieces(width):
        for s in range(samples):
            wide_rows[k, every(s, waves, samples), :] = filled(latent[s, :, at].astype(jnp.float32))
        whole = wide_rows[k].reshape(waves, samples, LANES)[:, :, : min(width, LANES)]
        for p in range(pieces):
            draws[p, :, :, at] = whole[p * own : (p + 1) * own].astype(draws.dtype)


def turn_rows(amp, rows, wide_rows, turned):
    waves, samples, width = amp.shape
    for k, at in lane_pieces(width):
        flat = amp[:, :, at].astype(jnp.float32).reshape(waves * samples, -1)
        wide_rows[k] = filled(flat)
        size = at.stop - at.start
        for s in range(samples):
            part = wide_rows[k, every(s, waves, samples), :].T[:size]
            turned[every(at.start * samples + s, size, samples), :] = part
    half = width // 2
    rows[:half] = turned[...].astype(rows.dtype).reshape(half, 2 * samples, waves)
    rows[half:] = jnp.zeros((GROUP // 2, 2 * samples, waves), rows.dtype)


def forward_kernel(
    axis, pieces, width, own, batch,
    coords, latents, length, amplitude_scale, label, kern, amp, rows, kept, pairs, trips,
    profile, latent, wide_rows, turned, dist, col_x, col_y, prof, later, draw, vec, prof_all, draws_all, stage, landed,
    in_send, in_recv, out_send, out_recv, bins, mark,
):
    total = pieces * width
    blocks = total // TILE
    samples = latent.shape[2]
    step = 64
    per = own // batch
    w = pl.program_id(0)
    sources, targets = (profile, latent), (prof_all, draws_all)
    begin_in, arrive_in, sent_in = inward(axis, pieces, batch, sources, targets, in_send, in_recv)
    begin_out, done_out = outward(axis, pieces, stage, landed, out_send, out_recv)

    marking = pltpu.make_async_copy(label, bins, mark)

    def read_marks():
        marking.wait()

        def over(c, _):
            pair = lax.shift_right_logical(bins[0, c * CHUNK], 1)
            pairs[c] = pair
            trips[c] = (bins[0, c * CHUNK + CHUNK - 1] - pair * 2) // GROUP + 1
            return 0

        lax.fori_loop(0, pairs.shape[0], over, 0)

    def entries(i, j, t, r, rows, c, cols):
        own_x = col_x[pl.ds(i * TILE + r, rows), :]
        square = jnp.concatenate([own_x] * (cols // LANES), axis=1) + prof[j, 0:1, c : c + cols]
        root = lax.rsqrt(square)
        return root * jnp.exp2(dist[t, r : r + rows, c : c + cols] * (root * root))

    @pl.when(w == 0)
    def _():
        hail(axis, pieces)
        marking.start()
        prepare(latents, length, amplitude_scale, latent, profile, wide_rows)
        spread_rows(col_x, lambda k: coords[0:1, k : k + LANES], total)
        spread_rows(col_y, lambda k: coords[1:2, k : k + LANES], total)
        open_batches(axis, pieces, batch, sources, targets, begin_in)

        def over_i(i, t0):
            def over_j(j, t):
                col = pl.ds(pl.multiple_of(j * TILE, TILE), TILE)
                x_c, y_c = coords[0:1, col], coords[1:2, col]
                for r in range(0, TILE, step):
                    row = pl.ds(pl.multiple_of(i * TILE + r, step), step)
                    dx = wide(col_x[row, :]) - x_c
                    dy = wide(col_y[row, :]) - y_c
                    dist[t, r : r + step, :] = (dx * dx + dy * dy) * (-math.log2(math.e))
                return t + 1

            return lax.fori_loop(i, blocks, over_j, t0)

        lax.fori_loop(0, blocks, over_i, 0)
        arrive_in(0)
        gather_pieces(later, lambda k: prof_all[k, 0], pieces, width)
        spread_rows(col_x, lambda k: later[k // TILE, 0:1, k % TILE : k % TILE + LANES], total)

    @pl.when(w > 0)
    def _():
        begin_out(w - 1)

    @pl.when(jnp.logical_and(w + 1 < own, lax.rem(w + 1, per) == 0))
    def _():
        arrive_in((w + 1) // per)

    @pl.when(w < own)
    def _():
        after = jnp.minimum(w + 1, own - 1)
        gather_pieces(prof, lambda k: prof_all[k, w], pieces, width)
        gather_pieces(later, lambda k: prof_all[k, after], pieces, width)
        gather_pieces(draw, lambda k: draws_all[k, w], pieces, width)
        kept[w] = prof[...]
        for j in range(blocks):
            split_scaled(vec, draw[j], prof[j, 1:2, :], j)
        sums = [None] * blocks
        for t, (i, j) in sorted(enumerate(tile_pairs(blocks)), key=lambda p: (-p[1][0], p[1][1])):
            if i == j:
                upper = entries(i, j, t, 0, LANES, 0, TILE)
                lower = entries(i, j, t, LANES, LANES, LANES, LANES)
                lower = jnp.concatenate([upper[:, LANES:].T, lower], axis=1)
                strips = [upper.astype(jnp.bfloat16), lower.astype(jnp.bfloat16)]
            else:
                strips = [
                    entries(i, j, t, r, step, 0, TILE).astype(jnp.bfloat16)
                    for r in range(0, TILE, step)
                ]
            tile = jnp.concatenate(strips, axis=0)
            kern[0, t] = tile
            multiply(sums, vec, tile, i, j)
            if j == blocks - 1:
                for k in range(0, TILE, LANES):
                    row = later[i, 0:1, k : k + LANES]
                    at = pl.ds(i * TILE + k, LANES)
                    col_x[at, :] = jnp.broadcast_to(row, (LANES, LANES)).T
        sums = joined(sums, lambda j: prof[j, 1:2, :], samples)
        keep_pieces(stage, w, sums, pieces, width)

    @pl.when(w == own)
    def _():
        read_marks()
        sent_in()
        done_out()
        whole = landed[...].reshape(amp.shape)
        amp[...] = whole
        turn_rows(whole, rows, wide_rows, turned)


def backward_kernel(
    axis, pieces, width, own, batch, slots,
    kern, grad, prof, out,
    tiles, turned, draw, vec, grad_all, stage, landed, load, in_send, in_recv, out_send, out_recv,
):
    total = pieces * width
    blocks = total // TILE
    samples = grad.shape[2]
    w = pl.program_id(0)
    begin_in, arrive_in, sent_in = inward(axis, pieces, batch, (grad,), (grad_all,), in_send, in_recv)
    begin_out, done_out = outward(axis, pieces, stage, landed, out_send, out_recv)

    def loading(n):
        slot = lax.rem(n, slots)
        return pltpu.make_async_copy(kern.at[n], tiles.at[slot], load.at[slot])

    @pl.when(w == 0)
    def _():
        hail(axis, pieces)
        for n in range(slots):
            loading(n).start()
        open_batches(axis, pieces, batch, (grad,), (grad_all,), begin_in)

    @pl.when(w > 0)
    def _():
        begin_out(w - 1)

    @pl.when(jnp.logical_and(w > 0, w - 1 + slots < own))
    def _():
        loading(w - 1 + slots).start()

    @pl.when(jnp.logical_and(w < own, lax.rem(w, own // batch) == 0))
    def _():
        arrive_in(w // (own // batch))

    @pl.when(w < own)
    def _():
        gather_pieces(draw, lambda k: grad_all[k, w], pieces, width)
        for j in range(blocks):
            split_scaled(vec, draw[j], prof[w, j, 1:2, :], j)
        loading(w).wait()
        slot = lax.rem(w, slots)
        sums = [None] * blocks
        for t, (i, j) in enumerate(tile_pairs(blocks)):
            tile = tiles[slot, t]
            sums[j] = add(sums[j], dot(vec[i], tile, NN))
            if j > i:
                turned[t] = tile.T
                sums[i] = add(sums[i], dot(vec[j], turned[t], NN))
        sums = joined(sums, lambda j: prof[w, j, 1:2, :], samples)
        keep_pieces(stage, w, sums, pieces, width)

    @pl.when(w == own)
    def _():
        sent_in()
        done_out()
        out[...] = landed[...]


def own_bins(label, at, start, samples):
    return jnp.broadcast_to(label[:, at], (samples, CHUNK)) - start


def field_group(samples, rows, data, own, pair):
    part = jnp.concatenate([rows[pair + i] for i in range(GROUP // 2)], axis=0)
    full = dot(part, data, NT)
    total = jnp.zeros((samples, CHUNK), jnp.float32)
    for b in range(GROUP):
        total = total + jnp.where(own == b, full[b * samples : (b + 1) * samples, :], 0.0)
    return total


def sums_group(value, data, own):
    full = jnp.concatenate([jnp.where(own == b, value, 0.0) for b in range(GROUP)], axis=0)
    return dot(full.astype(jnp.bfloat16), data, NN)


def chunk_at(c):
    return pl.ds(pl.multiple_of(c * CHUNK, CHUNK), CHUNK)


def fetch(source, held, sem):
    copy = pltpu.make_async_copy(source, held, sem)
    copy.start()
    copy.wait()


def finish_kernel(pulled, latent, out, wide_rows):
    samples, waves, width = latent.shape
    spread_samples(wide_rows, pulled)
    for k, at in lane_pieces(width):
        for s in range(samples):
            value = wide_rows[k, every(s, waves, samples), :][:, : min(width, LANES)]
            out[s, :, at] = value + latent[s, :, at].astype(jnp.float32)


def rest_field_kernel(samples, chunks, pairs, trips, spread, label, basis, extra, held, sem, rows, tag):
    extra[...] = jnp.zeros_like(extra)

    def over(c, _):
        start, count = pairs[c] * 2, trips[c]

        @pl.when(count > 1)
        def _():
            fetch(basis.at[chunk_at(c)], held, sem)
            fetch(label.at[:, chunk_at(c)], tag, sem)
            fetch(spread, rows, sem)

            def more(k, total):
                first = start + k * GROUP
                own = own_bins(tag, slice(None), first, samples)
                return total + field_group(samples, rows, held[...], own, first // 2)

            extra[c] = lax.fori_loop(1, count, more, jnp.zeros((samples, CHUNK), jnp.float32))

        return 0

    lax.fori_loop(0, chunks, over, 0)


def rest_sums_kernel(
    samples, chunks, halves, per,
    pairs, trips, terms, weight, label, amp, yield_norm, basis, grad,
    sums, wide_rows, held, sem,
):
    waves, _, width = amp.shape
    sums[...] = jnp.zeros_like(sums)

    def put(start, term):
        sums[pl.ds(pl.multiple_of(start * samples, 2 * samples), GROUP * samples), :] += term

    def over(c, _):
        start, count = pairs[c] * 2, trips[c]
        put(start, terms[c])

        @pl.when(count > 1)
        def _():
            fetch(basis.at[chunk_at(c)], held, sem)
            part, at = c // per, chunk_at(c % per)
            value = weight[part // halves, part % halves, :, at].astype(jnp.float32)

            def more(k, _):
                first = start + k * GROUP
                own = own_bins(label, chunk_at(c), first, samples)
                put(first, sums_group(value, held[...], own))
                return 0

            lax.fori_loop(1, count, more, 0)

        return 0

    lax.fori_loop(0, chunks, over, 0)
    spread_samples(wide_rows, amp)
    for k, at in lane_pieces(width):
        size = at.stop - at.start
        norm = filled(yield_norm[:, at]) * (2.0 / samples)
        for s in range(samples):
            mine = every(s, waves, samples)
            part = sums[every(at.start * samples + s, size, samples), :]
            part = jnp.concatenate([part] * (LANES // size), axis=0).T
            wide_rows[k, mine, :] = part + wide_rows[k, mine, :] * norm
        whole = wide_rows[k].reshape(waves, samples, LANES)
        grad[:, :, at] = whole[:, :, :size].astype(grad.dtype)


def events_kernel(
    axis, count, samples, halves, per,
    pairs, rows, label, extra, basis, terms, weight,
    held, partial, landed, send, recv, load,
):
    me = lax.axis_index(axis)
    parts = count * halves
    size = per * CHUNK

    def place(n):
        return lax.rem(me + 1 + lax.rem(n, count), count), n // count

    def loading(n):
        p, h = place(n)
        at = pl.ds(pl.multiple_of((p * halves + h) * size, size), size)
        return pltpu.make_async_copy(basis.at[at], held.at[at], load.at[n])

    def reducing(h, d):
        p = lax.rem(me + 1 + d, count)
        return remote(axis, p, partial.at[p, h], landed.at[d, h], send.at[0, h, d], recv.at[0, h, d])

    def sharing(h, d):
        p = lax.rem(me + 1 + d, count)
        return remote(axis, p, weight.at[me, h], weight.at[me, h], send.at[1, h, d], recv.at[1, h, d])

    ahead = min(2, parts)
    for n in range(ahead):
        loading(n).start()
    hail(axis, count)
    hear(count)

    def field(n, _):
        p, h = place(n)
        loading(n).wait()

        @pl.when(n + ahead < parts)
        def _():
            loading(n + ahead).start()

        for k in range(per):
            c = (p * halves + h) * per + k
            pair = pairs[c]
            own = own_bins(label, chunk_at(c), pair * 2, samples)
            total = extra[c] + field_group(samples, rows, held[chunk_at(c), :], own, pair)
            partial[p, h, :, k * CHUNK : (k + 1) * CHUNK] = total.astype(partial.dtype)

        @pl.when(lax.rem(n, count) < count - 1)
        def _():
            reducing(h, lax.rem(n, count)).start()

        return 0

    def sums(p, h):
        for k in range(per):
            c = (p * halves + h) * per + k
            own = own_bins(label, chunk_at(c), pairs[c] * 2, samples)
            value = weight[p, h, :, k * CHUNK : (k + 1) * CHUNK].astype(jnp.float32)
            terms[c] = sums_group(value, held[chunk_at(c), :], own)

    lax.fori_loop(0, parts, field, 0)

    def first(h, _):
        for d in range(count - 1):
            reducing(h, d).wait_recv()
        for k in range(per):
            at = slice(k * CHUNK, (k + 1) * CHUNK)
            total = partial[me, h, :, at].astype(jnp.float32)
            for d in range(count - 1):
                total = total + landed[d, h, :, at].astype(jnp.float32)
            weight[me, h, :, at] = (-2.0 * total / (1.0 + total * total) / samples).astype(weight.dtype)
        for d in range(count - 1):
            sharing(h, d).start()
        sums(me, h)
        return 0

    lax.fori_loop(0, halves, first, 0)

    def second(n, _):
        h, d = n // (count - 1), lax.rem(n, count - 1)
        sharing(h, d).wait_recv()
        sums(lax.rem(me + count - 1 - d, count), h)
        return 0

    lax.fori_loop(0, halves * (count - 1), second, 0)
    for h in range(halves):
        for d in range(count - 1):
            reducing(h, d).wait_send()
            sharing(h, d).wait_send()


def hail(axis, count):
    me, peers = around(axis, count)
    for peer in peers:
        pl.semaphore_signal(
            pltpu.get_barrier_semaphore(), inc=1, device_id={axis: peer}, device_id_type=MESH
        )


def hear(count):
    pl.semaphore_wait(pltpu.get_barrier_semaphore(), count - 1)


def params(**more):
    return pltpu.CompilerParams(
        dimension_semantics=("arbitrary",), vmem_limit_bytes=60 << 20, **more
    )


def shards(count, splits, latent, basis, event_bin, length, amplitude_scale, yield_norm, bin_coords):
    samples, waves, width = latent.shape
    total = bin_coords.shape[1]
    own = waves // count
    blocks = total // TILE
    tiles = blocks * (blocks + 1) // 2
    f32, bf16 = jnp.float32, jnp.bfloat16

    sheets = pltpu.VMEM((max(width // LANES, 1), waves * samples, LANES), f32)
    turned_shape = jax.ShapeDtypeStruct((waves, samples, width), bf16)

    def local(body, name, out_shape, in_specs, out_specs, scratch_shapes):
        return pl.pallas_call(
            body,
            out_shape=out_shape,
            in_specs=in_specs,
            out_specs=out_specs,
            scratch_shapes=scratch_shapes,
            compiler_params=pltpu.CompilerParams(vmem_limit_bytes=57 << 20),
            name=name,
        )

    vmem = pl.BlockSpec(memory_space=pltpu.VMEM)
    batch = math.gcd(own, BATCHES)
    piece = jax.ShapeDtypeStruct((count, own, samples, width), bf16)
    kern_spec = pl.BlockSpec((1, tiles, TILE, TILE), lambda w: (jnp.minimum(w, own - 1), 0, 0, 0))
    stages = [
        pltpu.VMEM((own, count, samples, width), bf16),
        pltpu.VMEM((count, own, samples, width), bf16),
    ]

    def semaphores(arrays):
        return [
            pltpu.SemaphoreType.DMA((arrays,)),
            pltpu.SemaphoreType.DMA((arrays, batch)),
            pltpu.SemaphoreType.DMA,
            pltpu.SemaphoreType.DMA,
        ]

    events = basis.shape[0]
    chunks = events // CHUNK
    smem = pl.BlockSpec(memory_space=pltpu.SMEM)
    anywhere = pl.BlockSpec(memory_space=pltpu.HBM)
    marks = jax.ShapeDtypeStruct((chunks,), jnp.int32)
    kern, amp, amp_rows, kept, pairs, trips = pl.pallas_call(
        functools.partial(forward_kernel, "event", count, width, own, batch),
        out_shape=(
            jax.ShapeDtypeStruct((own, tiles, TILE, TILE), bf16),
            turned_shape,
            jax.ShapeDtypeStruct(((width + GROUP) // 2, 2 * samples, waves), bf16),
            jax.ShapeDtypeStruct((own, blocks, 2, TILE), f32),
            marks,
            marks,
        ),
        grid=(own + 1,),
        in_specs=[vmem, vmem, vmem, vmem, anywhere],
        out_specs=(kern_spec, vmem, vmem, vmem, smem, smem),
        scratch_shapes=[
            pltpu.VMEM((count, own, 2, width), f32),
            pltpu.VMEM((count, own, samples, width), bf16),
            sheets,
            pltpu.VMEM((width * samples, waves), f32),
            pltpu.VMEM((tiles, TILE, TILE), f32),
            pltpu.VMEM((total, LANES), f32),
            pltpu.VMEM((total, LANES), f32),
            pltpu.VMEM((blocks, 2, TILE), f32),
            pltpu.VMEM((blocks, 2, TILE), f32),
            pltpu.VMEM((blocks, samples, TILE), bf16),
            pltpu.VMEM((blocks, 2 * samples, TILE), bf16),
            pltpu.VMEM((count, own, 2, width), f32),
            pltpu.VMEM((count, own, samples, width), bf16),
        ]
        + stages
        + semaphores(2)
        + [pltpu.SMEM(event_bin.shape, jnp.int32), pltpu.SemaphoreType.DMA],
        compiler_params=params(collective_id=0, has_side_effects=True),
        name="kern_forward",
    )(bin_coords, latent, length, amplitude_scale, event_bin)

    halves = math.gcd(chunks // splits, HALVES)
    per = chunks // splits // halves
    one = [pltpu.VMEM((CHUNK, waves), bf16), pltpu.SemaphoreType.DMA]
    extra = local(
        functools.partial(rest_field_kernel, samples, chunks),
        "rest_field",
        jax.ShapeDtypeStruct((chunks, samples, CHUNK), f32),
        [smem, smem, anywhere, anywhere, anywhere],
        vmem,
        one + [pltpu.VMEM(amp_rows.shape, bf16), pltpu.VMEM((1, CHUNK), jnp.int32)],
    )(pairs, trips, amp_rows, event_bin, basis)
    shared = (splits, halves, samples, per * CHUNK)
    terms, weight = pl.pallas_call(
        functools.partial(events_kernel, "wave", splits, samples, halves, per),
        out_shape=(
            jax.ShapeDtypeStruct((chunks, GROUP * samples, waves), f32),
            jax.ShapeDtypeStruct(shared, bf16),
        ),
        in_specs=[smem, vmem, vmem, vmem, anywhere],
        out_specs=(vmem, vmem),
        scratch_shapes=[
            pltpu.VMEM((events, waves), bf16),
            pltpu.VMEM(shared, bf16),
            pltpu.VMEM((splits - 1,) + shared[1:], bf16),
            pltpu.SemaphoreType.DMA((2, halves, splits - 1)),
            pltpu.SemaphoreType.DMA((2, halves, splits - 1)),
            pltpu.SemaphoreType.DMA((splits * halves,)),
        ],
        compiler_params=pltpu.CompilerParams(
            collective_id=2, has_side_effects=True, vmem_limit_bytes=57 << 20
        ),
        name="events",
    )(pairs, amp_rows, event_bin, extra, basis)
    grad = local(
        functools.partial(rest_sums_kernel, samples, chunks, halves, per),
        "rest_sums",
        turned_shape,
        [smem, smem] + [vmem] * 5 + [anywhere],
        vmem,
        [pltpu.VMEM(((width + GROUP) * samples, waves), f32), sheets] + one,
    )(pairs, trips, terms, weight, event_bin, amp, yield_norm, basis)
    slots = min(own, AHEAD)
    pulled = pl.pallas_call(
        functools.partial(backward_kernel, "event", count, width, own, batch, slots),
        out_shape=piece,
        grid=(own + 1,),
        in_specs=[anywhere, vmem, vmem],
        out_specs=vmem,
        scratch_shapes=[
            pltpu.VMEM((slots, tiles, TILE, TILE), bf16),
            pltpu.VMEM((tiles, TILE, TILE), bf16),
            pltpu.VMEM((blocks, samples, TILE), bf16),
            pltpu.VMEM((blocks, 2 * samples, TILE), bf16),
            pltpu.VMEM((count, own, samples, width), bf16),
        ]
        + stages
        + [pltpu.SemaphoreType.DMA((slots,))]
        + semaphores(1),
        compiler_params=params(collective_id=1, has_side_effects=True),
        name="kern_backward",
    )(kern, grad.reshape(count, own, samples, width), kept)
    return local(
        finish_kernel,
        "finish",
        jax.ShapeDtypeStruct(latent.shape, f32),
        [vmem, vmem],
        vmem,
        [sheets],
    )(pulled.reshape(waves, samples, width), latent)


def solution(mesh):
    placed = (
        P(None, "wave", "event"),
        P("event", "wave"),
        P("event", None),
        P("wave", "event"),
        P("wave", "event"),
        P("wave", "event"),
        P(),
    )
    return jax.shard_map(
        functools.partial(shards, mesh.shape["event"], mesh.shape["wave"]),
        mesh=mesh,
        in_specs=placed,
        out_specs=P(None, "wave", "event"),
        check_vma=False,
    )
```
